512 devices in a mesh: seq: 128 (over z_hi, x, y), slab: 4 (over z_lo, core).
Axes of the slice: x: 4, y: 8, z: 8 (z_hi: 4, z_lo: 2; z = z_hi * 2 + z_lo), core: 2. Of those that a mesh axis runs over, the one named last changes fastest.
Arguments:
- hidden: bfloat16 [12288, 5120], P('seq', 'slab'), may hold values from -130 to 130, as said below
- tangent: bfloat16 [12288, 5120], P('seq', 'slab'), may hold values from -6 to 6
- mod_shift: float32 [5120], P('slab'), may hold values from -2 to 2
- mod_scale: float32 [5120], P('slab'), may hold values from -1.5 to 1.5
- head_weight: bfloat16 [64, 5120], P(None, 'slab'), may hold values from -0.078125 to 0.078125
- head_bias: float32 [64], replicated, may hold values from -2 to 2
- in_weight: bfloat16 [3, 3, 3, 16, 384], replicated, may hold values from -0.3125 to 0.3125
- in_bias: float32 [384], replicated, may hold values from -2 to 2
- norm_gain: float32 [384], replicated, may hold values from 0.1 to 1.9
- mid_weight: bfloat16 [3, 3, 3, 384, 384], P(None, None, None, 'slab'), may hold values from -0.0625 to 0.0625
Outputs:
- features_tangent: bfloat16 [128, 2, 48, 4, 384], P('seq', None, 'slab')
The draws below stay inside these ranges and needn't reach their ends.
Inputs may be any that keep to these rules, and one draw needn't show every extreme that they name: hidden states of the transformer's last block.
All inputs are finite; a program needn't handle non-finite values.
Results may differ from the reference program's by a relative error of at most 0.008.
Values may be sent and summed in bfloat16 or wider, within the bound.
A program may use at most 64 MiB of HBM per device.

```python
import jax
import jax.numpy as jnp
from jax import lax

D = 5120
ZC = 16
CH = 384
CG = 8
FR_DEV = 2
HT = 24
CT = 2
WT = 16
FRAMES = 32
TOKENS = 12288
HL = 48
WL = 32
N_SEQ = 128


def draw_hidden(key, part):
    key_a, key_b, key_c = jax.random.split(jax.random.fold_in(key, 7), 3)
    column_scale = 10.0 ** jax.random.uniform(key_b, (D,), jnp.float32) * 3.0 ** (jnp.arange(D, dtype=jnp.float32) / D)
    row_scale = 10.0 ** jax.random.uniform(key_c, (TOKENS, 1), jnp.float32)
    sample = jnp.clip(jax.random.normal(key_a, (TOKENS, D), jnp.float32), -6.0, 6.0)
    return (0.05 * sample * column_scale * row_scale).astype(jnp.bfloat16)


def levels(rng, shape, cuts, least, high):
    factor_of, own = 1.0, jax.random.fold_in(rng, 6)
    for axis_at, shards_of in cuts:
        heights = jnp.exp(jax.random.uniform(jax.random.fold_in(own, axis_at), (shards_of,), jnp.float32, least / len(cuts), high / len(cuts)))
        factor_of = factor_of * jnp.repeat(heights, shape[axis_at] // shards_of).reshape([-1 if axis == axis_at else 1 for axis in range(len(shape))])
    return factor_of


def centred(own_key, shape, scale, most, shards=(), kind=jnp.bfloat16):
    drawn = jax.random.normal(own_key, shape, jnp.float32) * scale
    if len(shards) > 0:
        drawn = levels(own_key, shape, shards, -0.22, 0.18) * drawn
    return jnp.clip(drawn, min=-most, max=most).astype(kind)


def setup_inputs(seed: int = 0) -> dict:
    key_of = jax.random.split(jax.random.key(seed), 11)
    return {
        "hidden": draw_hidden(jax.random.fold_in(key_of[10], 71), 0),
        "tangent": centred(key_of[1], (TOKENS, D), 1.0, 6.0, ((0, 128), (1, 4))),
        "mod_shift": centred(key_of[2], (D,), 0.5, 2.0, ((0, 4),), jnp.float32),
        "mod_scale": centred(key_of[3], (D,), 0.5, 1.5, ((0, 4),), jnp.float32),
        "head_weight": centred(key_of[4], (4 * ZC, D), D ** -0.5, 0.078125, ((1, 4),)),
        "head_bias": centred(key_of[5], (4 * ZC,), 0.5, 2.0, (), jnp.float32),
        "in_weight": centred(key_of[6], (3, 3, 3, ZC, CH), (27 * ZC) ** -0.5, 0.3125),
        "in_bias": centred(key_of[7], (CH,), 0.5, 2.0, (), jnp.float32),
        "norm_gain": jnp.clip(1.0 + 0.18 * jax.random.normal(key_of[8], (CH,), jnp.float32), 0.1, 1.9),
        "mid_weight": centred(key_of[9], (3, 3, 3, CH, CH), (27 * CH) ** -0.5, 0.0625, ((3, 4),)),
    }


def norm_tangent(features, dfeatures, norm_gain):
    scale_inv = lax.rsqrt(lax.optimization_barrier(jnp.mean(features * features, axis=-1, keepdims=True)) + 1e-06)
    along = lax.optimization_barrier(jnp.mean(features * dfeatures, axis=-1, keepdims=True))
    normed_feat = norm_gain * features * scale_inv
    tangent_feat = norm_gain * scale_inv * (dfeatures - features * scale_inv * scale_inv * along)
    sigmoid_u = jax.nn.sigmoid(normed_feat)
    return (sigmoid_u * (1.0 + normed_feat * (1.0 - sigmoid_u)) * tangent_feat).astype(jnp.bfloat16)

def reference(hidden, tangent, mod_shift, mod_scale, head_weight, head_bias, in_weight, in_bias, norm_gain, mid_weight):
    states = hidden.astype(jnp.float32)
    tangents = tangent.astype(jnp.float32)
    token_mean = lax.optimization_barrier(jnp.sum(states, axis=1, keepdims=True)) / D
    variance = lax.optimization_barrier(jnp.sum(states * states, axis=1, keepdims=True)) / D - token_mean * token_mean
    inverse = lax.rsqrt(variance + 1e-06)
    mean_tangent = lax.optimization_barrier(jnp.sum(tangents, axis=1, keepdims=True)) / D
    project = inverse * (lax.optimization_barrier(jnp.sum(states * tangents, axis=1, keepdims=True)) / D - token_mean * mean_tangent)
    normed = (states - token_mean) * inverse
    dnormed = inverse * (tangents - mean_tangent - normed * project)
    scaling = 1.0 + mod_scale
    modulated = (normed * scaling + mod_shift).astype(jnp.bfloat16)
    dmodulated = (dnormed * scaling).astype(jnp.bfloat16)
    head_cols = head_weight.T
    patches = (jnp.dot(modulated, head_cols, preferred_element_type=jnp.float32) + head_bias).astype(jnp.bfloat16)
    dpatches = jnp.dot(dmodulated, head_cols, preferred_element_type=jnp.float32).astype(jnp.bfloat16)
    packed = jnp.concatenate([patches, dpatches], axis=1)
    token_grid = packed.reshape(FRAMES, HT, WT, 2, 2, 2, ZC)
    latents = token_grid.transpose(3, 0, 1, 4, 2, 5, 6).reshape(2, FRAMES, HL, WL, ZC)
    padded = jnp.pad(latents, ((0, 0), (2, 0), (1, 1), (1, 1), (0, 0)))
    pieces = []
    for frame_tap in range(3):
        for row_tap in range(3):
            for col_tap in range(3):
                pieces.append(padded[:, frame_tap:frame_tap + FRAMES, row_tap:row_tap + HL, col_tap:col_tap + WL, :])
    stacked = jnp.concatenate(pieces, axis=-1).astype(jnp.float32)
    conv_pair = jnp.dot(stacked, in_weight.reshape(27 * ZC, CH).astype(jnp.float32))
    features = conv_pair[0] + in_bias
    dfeatures = conv_pair[1]
    act_tangent = norm_tangent(features, dfeatures, norm_gain)
    tangent_pad = jnp.pad(act_tangent, ((2, 0), (1, 1), (1, 1), (0, 0)))
    running = jnp.zeros((FRAMES, HL, WL, CH), jnp.float32)
    for frame_tap in range(3):
        for row_tap in range(3):
            for col_tap in range(3):
                window = tangent_pad[frame_tap:frame_tap + FRAMES, row_tap:row_tap + HL, col_tap:col_tap + WL, :]
                running = running + jnp.dot(window.astype(jnp.float32), mid_weight[frame_tap, row_tap, col_tap].astype(jnp.float32))
    grid_tangent = (running + dfeatures).astype(jnp.bfloat16)
    tiled = grid_tangent.reshape(N_SEQ // CG, FR_DEV, HL, CG, 2 * CT, CH).transpose(0, 3, 1, 2, 4, 5)
    tiled = tiled.reshape(N_SEQ, FR_DEV, HL, 2 * CT, CH)
    return jnp.roll(tiled, CG // 2, axis=0)
```

```python
import jax
import jax.numpy as jnp
from jax import lax
from jax.experimental import pallas as pl
from jax.experimental.pallas import tpu as pltpu
from jax.sharding import PartitionSpec as P

D = 5120
CH = 384
CG = 8
GROUPS = 16
SLABS = 4
TOK = 96
DS = D // SLABS
SHARE = CH // SLABS
F32 = jnp.float32
BF16 = jnp.bfloat16
MESH = pl.DeviceIdType.MESH
NT = (((1,), (1,)), ((), ()))


def lanes_of(shape):
    return lax.broadcasted_iota(jnp.int32, shape, len(shape) - 1)


def head_partials(xv, dxv, hwv, scale_ref, shift_ref, send):
    x = xv[...]
    dx = dxv[...]
    xf = x.astype(F32)
    dxf = dx.astype(F32)
    sums = [
        jnp.sum(xf, axis=1, keepdims=True),
        jnp.sum(xf * xf, axis=1, keepdims=True),
        jnp.sum(dxf, axis=1, keepdims=True),
        jnp.sum(xf * dxf, axis=1, keepdims=True),
    ]
    lane = lanes_of((TOK, 128))
    moments = jnp.zeros((TOK, 128), F32)
    for k, value in enumerate(sums):
        moments = jnp.where(lane == k, value, moments)
    moments = jnp.concatenate([moments, jnp.zeros((128 - TOK, 128), F32)], axis=0)
    w = hwv[...]
    wf = w.astype(F32) * (1.0 + scale_ref[...].reshape(1, DS))
    hi = wf.astype(BF16)
    lo = (wf - hi.astype(F32)).astype(BF16)
    shift = shift_ref[...].reshape(1, DS)
    shift_hi = shift.astype(BF16).astype(F32)
    shift_mid = (shift - shift_hi).astype(BF16).astype(F32)
    shift_lo = shift - shift_hi - shift_mid
    row = lax.broadcasted_iota(jnp.int32, (16, DS), 0)
    extra = jnp.where(row == 0, 1.0, 0.0)
    extra = jnp.where(row == 1, shift_hi, extra)
    extra = jnp.where(row == 2, shift_mid, extra)
    extra = jnp.where(row == 3, shift_lo, extra).astype(BF16)
    both = jnp.concatenate([x, dx, extra], axis=0)
    split = jnp.concatenate([hi, lo], axis=0)
    prod = lax.dot_general(both, split, NT, preferred_element_type=F32)
    prod = prod + pltpu.roll(prod, 64, 1)
    twice = jnp.concatenate([w, w], axis=0)
    shifted = lax.dot_general(extra, twice, NT, preferred_element_type=F32)
    lane1 = lanes_of((8, 128))
    ones_row = jnp.broadcast_to(prod[2 * TOK : 2 * TOK + 1], (8, 128))
    shift_row = jnp.broadcast_to(shifted[1:2] + shifted[2:3] + shifted[3:4], (8, 128))
    send[0:TOK, :] = jnp.where(lane < 64, prod[0:TOK], prod[TOK : 2 * TOK])
    send[TOK : TOK + 8, :] = jnp.transpose(moments)[0:8]
    send[TOK + 8 : TOK + 16, :] = jnp.where(lane1 < 64, ones_row, shift_row)


def head_finish(total, bias):
    part = total[0:TOK]
    moments = jnp.concatenate([total[TOK : TOK + 8], jnp.zeros((120, 128), F32)], axis=0)
    moments = jnp.transpose(moments)[0:TOK]
    const = total[TOK + 8 : TOK + 9]
    mean = moments[:, 0:1] / D
    variance = moments[:, 1:2] / D - mean * mean
    inverse = lax.rsqrt(variance + 1e-06)
    mean_tangent = moments[:, 2:3] / D
    project = inverse * (moments[:, 3:4] / D - mean * mean_tangent)
    lane = lanes_of((TOK, 128))
    lane1 = lanes_of((1, 128))
    turned = pltpu.roll(jnp.broadcast_to(const, (8, 128)), 64, 1)[0:1]
    weight_sum = jnp.where(lane1 < 64, const, turned)
    shift_term = turned
    value = inverse * (part - jnp.where(lane < 64, mean, mean_tangent) * weight_sum)
    primal = value + shift_term + bias
    tangent = value - inverse * project * pltpu.roll(value, 64, 1)
    return jnp.where(lane < 64, primal, tangent).astype(BF16)


def kernel(
    x_any, dx_any, shift_ref, scale_ref, hw_any, bias_ref, inw_any, inb_ref, gain_ref, mid_any,
    out_ref,
    xv, dxv, hwv, inwv, part, part_in, tiles, tiles_in, block, grid, pairs, wide, acts, resid,
    midw, sums_out, sums_in,
    load_sem, mid_sem, b_send, b_recv, c_send, c_recv, g_send, g_recv, m_send, m_recv, r_send, r_recv,
):
    seq = lax.axis_index("seq")
    slab = lax.axis_index("slab")
    y = lax.rem(seq, CG)
    group = lax.div(seq, CG)
    core = lax.rem(slab, 2)
    half = lax.div(slab, 2)
    late = (y < 4).astype(jnp.int32)
    tile_group = lax.rem(group - late + GROUPS, GROUPS)
    column = lax.rem(y + 4, CG)

    loads = [
        pltpu.make_async_copy(x_any, xv, load_sem.at[0]),
        pltpu.make_async_copy(dx_any, dxv, load_sem.at[1]),
        pltpu.make_async_copy(hw_any, hwv, load_sem.at[2]),
        pltpu.make_async_copy(inw_any, inwv, load_sem.at[3]),
    ]
    for copy in loads:
        copy.start()

    barrier = pltpu.get_barrier_semaphore()
    for k in range(1, SLABS):
        pl.semaphore_signal(
            barrier, inc=1, device_id=(seq, lax.rem(slab + k, SLABS)), device_id_type=MESH
        )
    for k in range(1, CG):
        pl.semaphore_signal(
            barrier, inc=1, device_id=(group * CG + lax.rem(y + k, CG), slab), device_id_type=MESH
        )
    for k in (1, 2, 3, GROUPS - 3, GROUPS - 2, GROUPS - 1):
        pl.semaphore_signal(
            barrier, inc=1, device_id=(lax.rem(group + k, GROUPS) * CG + y, slab), device_id_type=MESH
        )

    spare = pl.multiple_of(192 - 192 * half, 64)
    midw[:, pl.ds(spare, 64), :] = jnp.zeros((27, 64, CH), BF16)
    own_rows = pl.multiple_of(half * 64 + core * SHARE, 32)
    mid_copy = pltpu.make_async_copy(mid_any, midw.at[:, pl.ds(own_rows, SHARE), :], mid_sem)
    mid_copy.start()

    loads[0].wait()
    loads[1].wait()
    loads[2].wait()
    head_partials(xv, dxv, hwv, scale_ref, shift_ref, part)

    pl.semaphore_wait(barrier, 3 + 7 + 6)

    b_copies = []
    for k in (2, 3, 1):
        b_copies.append(
            pltpu.make_async_remote_copy(
                src_ref=part,
                dst_ref=part_in.at[k - 1],
                send_sem=b_send.at[k - 1],
                recv_sem=b_recv.at[k - 1],
                device_id=(seq, lax.rem(slab + k, SLABS)),
                device_id_type=MESH,
            )
        )
        b_copies[-1].start()

    loads[3].wait()
    for par in range(2):
        for q in range(2):
            for a in range(3):
                for i in range(4):
                    for j in range(4):
                        tap_row, tap_col = (i - par, j - q)
                        cell = (i // 2) * 8 + (j // 2) * 4 + (i % 2) * 2 + j % 2
                        rows = slice(a * 256 + cell * 16, a * 256 + cell * 16 + 16)
                        if 0 <= tap_row < 3 and 0 <= tap_col < 3:
                            piece = inwv[a * 9 + tap_row * 3 + tap_col]
                        else:
                            piece = jnp.zeros((16, CH), BF16)
                        wide[par * 2 + q, rows, :] = piece

    quarter = lax.rem(y, 4)
    is_main = lax.rem(quarter, 2) == core
    row = lax.broadcasted_iota(jnp.int32, (256, TOK), 0)
    token = lax.broadcasted_iota(jnp.int32, (256, TOK), 1)
    t = row & 7
    col = 2 * (((row >> 5) + 4) & 7) - 1 + ((row >> 3) & 3)
    edge_row = jnp.where(t == 0, 5, jnp.where(t == 7, 0, -1))
    main_row = jnp.where((t == 0) | (t == 7), -1, t - 1)
    src_row = jnp.where(is_main, main_row, edge_row)
    hit = (src_row >= 0) & (col >= 0) & (col < 16) & (token == src_row * 16 + col)
    pick = jnp.where(hit, 1.0, 0.0).astype(BF16)

    for copy in b_copies:
        copy.wait_recv()
    total = part[...] + part_in[0] + part_in[1] + part_in[2]
    patches = head_finish(total, bias_ref[...])
    spread = jnp.dot(pick, patches, preferred_element_type=F32).astype(BF16)
    tiles[...] = spread.reshape(CG, 32, 128)

    c_copies = []
    for k in (4, 3, 5, 2, 6, 1, 7):
        to = lax.rem(y + k, CG)
        c_copies.append(
            pltpu.make_async_remote_copy(
                src_ref=tiles.at[to],
                dst_ref=tiles_in.at[y],
                send_sem=c_send.at[k],
                recv_sem=c_recv.at[k],
                device_id=(group * CG + to, slab),
                device_id_type=MESH,
            )
        )
        c_copies[-1].start()
    tiles_in[y] = tiles[y]

    mid_swap = pltpu.make_async_remote_copy(
        src_ref=mid_any,
        dst_ref=midw.at[:, pl.ds(own_rows, SHARE), :],
        send_sem=m_send,
        recv_sem=m_recv,
        device_id=(seq, half * 2 + 1 - core),
        device_id_type=MESH,
    )
    mid_swap.start()

    for copy in c_copies:
        copy.wait_recv()
    t32 = lax.broadcasted_iota(jnp.int32, (32, 128), 0) & 7
    for f in range(2):
        for b in range(2):
            q = 2 * b + core
            main = tiles_in[4 * f + q].astype(F32)
            above = tiles_in[4 * f + jnp.maximum(q - 1, 0)].astype(F32)
            below = tiles_in[4 * f + jnp.minimum(q + 1, 3)].astype(F32)
            value = main
            value = value + jnp.where((t32 == 0) & (q > 0), above, 0.0)
            value = value + jnp.where((t32 == 7) & (q < 3), below, 0.0)
            block[f * 2 + b] = value.astype(BF16)

    g_copies = []
    for d in (2, 1, 0):
        g_copies.append(
            pltpu.make_async_remote_copy(
                src_ref=block,
                dst_ref=grid.at[2 - d],
                send_sem=g_send.at[d],
                recv_sem=g_recv.at[d],
                device_id=(lax.rem(group + d + late, GROUPS) * CG + y, slab),
                device_id_type=MESH,
            )
        )
    g_copies[0].start()
    g_copies[1].start()

    @pl.when(y < 4)
    def _():
        g_copies[2].start()
        g_copies[2].wait()

    @pl.when(y >= 4)
    def _():
        grid[2] = block[...]

    g_copies[0].wait_recv()
    g_copies[1].wait_recv()

    lane = lanes_of((2, 8, 128))
    low = lane < 64
    for slot in range(3):
        keep = jnp.where(tile_group >= 2 - slot, 1.0, 0.0)
        for f in range(2):
            cols = []
            turned = []
            cell = grid[slot, 2 * f : 2 * f + 2].astype(F32).reshape(2, 4, 8, 128) * keep
            for w in range(4):
                value = cell[:, w]
                cols.append(value)
                turned.append(pltpu.roll(value, 64, 2))
            for kind in range(2):
                for w in range(3):
                    if kind == 0:
                        pair = jnp.where(low, cols[w], turned[w + 1])
                    else:
                        pair = jnp.where(low, turned[w], cols[w + 1])
                    below = pltpu.roll(pair, 7, 1)
                    base = (slot * 2 + f) * 96 + kind * 48 + w * 16
                    pairs[base : base + 16, 0:128] = pair.reshape(16, 128).astype(BF16)
                    pairs[base : base + 16, 128:256] = below.reshape(16, 128).astype(BF16)

    window = jnp.concatenate([pairs[0:384], pairs[96:480], pairs[192:576]], axis=1)
    bias_in = inb_ref[...].reshape(1, 1, CH)
    gain = gain_ref[...].reshape(1, 1, CH)
    first_half = half == 0
    gain_own = jnp.where(first_half, gain[..., 0:256], gain[..., 128:384])
    shape = (4, 48, 1)
    frame = lax.broadcasted_iota(jnp.int32, shape, 0)
    line = lax.broadcasted_iota(jnp.int32, shape, 1)
    s = line & 7
    b_of = (line >> 3) & 1
    w_of = line >> 4
    for par in range(2):
        for q in range(2):
            conv = jnp.dot(window, wide[par * 2 + q], preferred_element_type=F32)
            conv = conv.reshape(4, 2, 48, CH)
            feat = conv[:, 0] + bias_in
            dfeat = conv[:, 1]
            scale_inv = lax.rsqrt(jnp.mean(feat * feat, axis=-1, keepdims=True) + 1e-06)
            along = jnp.mean(feat * dfeat, axis=-1, keepdims=True)
            feat_own = jnp.where(first_half, feat[..., 0:256], feat[..., 128:384])
            dfeat_own = jnp.where(first_half, dfeat[..., 0:256], dfeat[..., 128:384])
            normed = gain_own * feat_own * scale_inv
            tang = gain_own * scale_inv * (dfeat_own - feat_own * (scale_inv * scale_inv * along))
            sig = 1.0 / (1.0 + jnp.exp(-normed))
            act = sig * (1.0 + normed * (1.0 - sig)) * tang
            out_side = (frame < 2) & (tile_group == 0)
            if q == 0:
                out_side = out_side | ((w_of == 0) & (column == 0))
            else:
                out_side = out_side | ((w_of == 2) & (column == CG - 1))
            if par == 0:
                out_side = out_side | ((s == 0) & (2 * b_of + core == 0))
            else:
                out_side = out_side | ((s == 6) & (2 * b_of + core == 3))
            act = jnp.where(out_side, 0.0, act)
            moved = pltpu.roll(act.reshape(24, 8, 256), 7, 1).reshape(4, 3, 16, 256).astype(BF16)
            act = act.reshape(4, 3, 16, 256).astype(BF16)
            for w in range(3):
                acts[par, 2 * w + q] = act[:, w]
                acts[par + 2, 2 * w + q] = moved[:, w]
            keep = dfeat[2:4].reshape(2, 3, 2, 8, CH)
            keep = jnp.where(first_half, keep[:, :, 0], keep[:, :, 1])
            if par == 0:
                keep = pltpu.roll(keep.reshape(6, 8, CH), 7, 1).reshape(2, 3, 8, CH)
            for w in range(3):
                place = 2 * w + q - 1
                if 0 <= place < 4:
                    resid[1 - par, place] = keep[:, w]

    mid_copy.wait()
    mid_swap.wait()
    acc = jnp.zeros((256, CH), F32)
    for a in range(3):
        for b in range(3):
            for c in range(3):
                taken = acts[b : b + 2, c : c + 4, a : a + 2].reshape(256, 256)
                acc = acc + jnp.dot(taken, midw[a * 9 + b * 3 + c], preferred_element_type=F32)
    acc = acc.reshape(16, 2, 8, CH)
    mine = jnp.where(first_half, acc[:, 0], acc[:, 1])
    other = jnp.where(first_half, acc[:, 1], acc[:, 0])
    sums_out[...] = other.reshape(128, CH).astype(BF16)
    swap = pltpu.make_async_remote_copy(
        src_ref=sums_out,
        dst_ref=sums_in,
        send_sem=r_send,
        recv_sem=r_recv,
        device_id=(seq, (1 - half) * 2 + core),
        device_id_type=MESH,
    )
    swap.start()
    swap.wait_recv()
    final = mine.reshape(128, CH) + sums_in[...].astype(F32) + resid[...].reshape(128, CH)
    row = lax.broadcasted_iota(jnp.int32, (TOK, 128), 0)
    src = lax.broadcasted_iota(jnp.int32, (TOK, 128), 1)
    upper = row >= 48
    inner = jnp.where(upper, row - 48, row)
    want = ((inner >> 2) & 1) * 64 + (inner & 3) * 16 + jnp.where(upper, 8, 0) + (inner >> 3)
    order = jnp.where(src == want, 1.0, 0.0).astype(BF16)
    out_ref[...] = jnp.dot(order, final.astype(BF16), preferred_element_type=F32).astype(BF16)

    for copy in b_copies + c_copies + g_copies[0:2]:
        copy.wait_send()
    swap.wait_send()


def shards(hidden, tangent, mod_shift, mod_scale, head_weight, head_bias, in_weight, in_bias, norm_gain, mid_weight):
    any_spec = pl.BlockSpec(memory_space=pl.ANY)
    vmem = pl.BlockSpec(memory_space=pltpu.VMEM)
    bias = jnp.pad(head_bias, (0, 64)).reshape(1, 128)
    dma = pltpu.SemaphoreType.DMA
    out = pl.pallas_call(
        kernel,
        out_shape=jax.ShapeDtypeStruct((TOK, CH), BF16),
        in_specs=[any_spec, any_spec, vmem, vmem, any_spec, vmem, any_spec, vmem, vmem, any_spec],
        out_specs=vmem,
        scratch_shapes=[
            pltpu.VMEM((TOK, DS), BF16),
            pltpu.VMEM((TOK, DS), BF16),
            pltpu.VMEM((64, DS), BF16),
            pltpu.VMEM((27, 16, CH), BF16),
            pltpu.VMEM((TOK + 16, 128), F32),
            pltpu.VMEM((3, TOK + 16, 128), F32),
            pltpu.VMEM((CG, 32, 128), BF16),
            pltpu.VMEM((CG, 32, 128), BF16),
            pltpu.VMEM((4, 32, 128), BF16),
            pltpu.VMEM((3, 4, 32, 128), BF16),
            pltpu.VMEM((576, 256), BF16),
            pltpu.VMEM((4, 768, CH), BF16),
            pltpu.VMEM((4, 6, 4, 16, 256), BF16),
            pltpu.VMEM((2, 4, 2, 8, CH), F32),
            pltpu.VMEM((27, 256, CH), BF16),
            pltpu.VMEM((128, CH), BF16),
            pltpu.VMEM((128, CH), BF16),
            dma((4,)),
            dma,
            dma((3,)),
            dma((3,)),
            dma((CG,)),
            dma((CG,)),
            dma((3,)),
            dma((3,)),
            dma,
            dma,
            dma,
            dma,
        ],
        compiler_params=pltpu.CompilerParams(collective_id=0, has_side_effects=True),
        name="decode",
    )(
        hidden,
        tangent,
        mod_shift,
        mod_scale,
        head_weight,
        bias,
        in_weight.reshape(27, 16, CH),
        in_bias,
        norm_gain,
        mid_weight.reshape(27, SHARE, CH),
    )
    return out.reshape(1, 2, 12, 4, CH)


def solution(mesh):
    return jax.shard_map(
        shards,
        mesh=mesh,
        in_specs=(
            P("seq", "slab"),
            P("seq", "slab"),
            P("slab"),
            P("slab"),
            P(None, "slab"),
            P(),
            P(),
            P(),
            P(),
            P(None, None, None, "slab", None),
        ),
        out_specs=P("seq", None, "slab", None, None),
        check_vma=False,
    )
```

```python
import jax
import jax.numpy as jnp
from jax import lax
from jax.experimental import pallas as pl
from jax.experimental.pallas import tpu as pltpu
from jax.sharding import PartitionSpec as P

D = 5120
CH = 384
CG = 8
GROUPS = 16
SLABS = 4
TOK = 96
DS = D // SLABS
SHARE = CH // SLABS
F32 = jnp.float32
BF16 = jnp.bfloat16
MESH = pl.DeviceIdType.MESH
NT = (((1,), (1,)), ((), ()))


def lanes_of(shape):
    return lax.broadcasted_iota(jnp.int32, shape, len(shape) - 1)


def head_partials(xv, dxv, hwv, scale_ref, shift_ref, send):
    x = xv[...]
    dx = dxv[...]
    xf = x.astype(F32)
    dxf = dx.astype(F32)
    sums = [
        jnp.sum(xf, axis=1, keepdims=True),
        jnp.sum(xf * xf, axis=1, keepdims=True),
        jnp.sum(dxf, axis=1, keepdims=True),
        jnp.sum(xf * dxf, axis=1, keepdims=True),
    ]
    lane = lanes_of((TOK, 128))
    moments = jnp.zeros((TOK, 128), F32)
    for k, value in enumerate(sums):
        moments = jnp.where(lane == k, value, moments)
    moments = jnp.concatenate([moments, jnp.zeros((128 - TOK, 128), F32)], axis=0)
    w = hwv[...]
    wf = w.astype(F32) * (1.0 + scale_ref[...].reshape(1, DS))
    hi = wf.astype(BF16)
    lo = (wf - hi.astype(F32)).astype(BF16)
    shift = shift_ref[...].reshape(1, DS)
    shift_hi = shift.astype(BF16).astype(F32)
    shift_mid = (shift - shift_hi).astype(BF16).astype(F32)
    shift_lo = shift - shift_hi - shift_mid
    row = lax.broadcasted_iota(jnp.int32, (16, DS), 0)
    extra = jnp.where(row == 0, 1.0, 0.0)
    extra = jnp.where(row == 1, shift_hi, extra)
    extra = jnp.where(row == 2, shift_mid, extra)
    extra = jnp.where(row == 3, shift_lo, extra).astype(BF16)
    both = jnp.concatenate([x, dx, extra], axis=0)
    split = jnp.concatenate([hi, lo], axis=0)
    prod = lax.dot_general(both, split, NT, preferred_element_type=F32)
    prod = prod + pltpu.roll(prod, 64, 1)
    twice = jnp.concatenate([w, w], axis=0)
    shifted = lax.dot_general(extra, twice, NT, preferred_element_type=F32)
    lane1 = lanes_of((8, 128))
    ones_row = jnp.broadcast_to(prod[2 * TOK : 2 * TOK + 1], (8, 128))
    shift_row = jnp.broadcast_to(shifted[1:2] + shifted[2:3] + shifted[3:4], (8, 128))
    value = jnp.where(lane < 64, prod[0:TOK], prod[TOK : 2 * TOK])
    send[0:64, :] = value[16:80]
    send[64:80, :] = value[0:16]
    send[80:96, :] = value[80:96]
    send[TOK : TOK + 8, :] = jnp.transpose(moments)[0:8]
    send[TOK + 8 : TOK + 16, :] = jnp.where(lane1 < 64, ones_row, shift_row)


def head_finish(total, bias):
    part = jnp.concatenate([total[64:80], total[0:64], total[80:96]], axis=0)
    moments = jnp.concatenate([total[TOK : TOK + 8], jnp.zeros((120, 128), F32)], axis=0)
    moments = jnp.transpose(moments)[0:TOK]
    const = total[TOK + 8 : TOK + 9]
    mean = moments[:, 0:1] / D
    variance = moments[:, 1:2] / D - mean * mean
    inverse = lax.rsqrt(variance + 1e-06)
    mean_tangent = moments[:, 2:3] / D
    project = inverse * (moments[:, 3:4] / D - mean * mean_tangent)
    lane = lanes_of((TOK, 128))
    lane1 = lanes_of((1, 128))
    turned = pltpu.roll(jnp.broadcast_to(const, (8, 128)), 64, 1)[0:1]
    weight_sum = jnp.where(lane1 < 64, const, turned)
    shift_term = turned
    value = inverse * (part - jnp.where(lane < 64, mean, mean_tangent) * weight_sum)
    primal = value + shift_term + bias
    tangent = value - inverse * project * pltpu.roll(value, 64, 1)
    return jnp.where(lane < 64, primal, tangent).astype(BF16)


def kernel(
    x_any, dx_any, shift_any, scale_any, hw_any, bias_any, inw_any, inb_any, gain_any, mid_any,
    out_ref,
    xv, dxv, hwv, inwv, shift_ref, scale_ref, bias_ref, inb_ref, gain_ref, part, part_in, tiles, tiles_in, block, grid, pairs, wide, acts, resid,
    midw, sums_out, sums_in,
    near_sem, far_sem, load_sem, mid_sem, b_send, b_recv, c_send, c_recv, g_send, g_recv, m_send, m_recv, r_send, r_recv,
):
    seq = lax.axis_index("seq")
    slab = lax.axis_index("slab")
    y = lax.rem(seq, CG)
    group = lax.div(seq, CG)
    core = lax.rem(slab, 2)
    half = lax.div(slab, 2)
    late = (y < 4).astype(jnp.int32)
    tile_group = lax.rem(group - late + GROUPS, GROUPS)
    column = lax.rem(y + 4, CG)

    part_in[:, 0:64, :] = jnp.zeros((3, 64, 128), F32)
    barrier = pltpu.get_barrier_semaphore()
    z_hi = lax.div(group, 4)
    x = lax.rem(group, 4)

    def place(z_to, x_to, y_to):
        return (lax.rem(z_to, 4) * 4 + lax.rem(x_to, 4)) * CG + lax.rem(y_to, CG)

    beside_x = [(place(z_hi, x + k, y), slab) for k in (1, 3)]
    beside_z = [(place(z_hi + k, x, y), slab) for k in (1, 3)]
    beside_y = [(place(z_hi, x, y + k), slab) for k in (2, 6, 1, 7)]
    in_slab = [(seq, lax.rem(slab + k, SLABS)) for k in range(1, SLABS)]
    for device in beside_z + beside_y + beside_x + in_slab:
        pl.semaphore_signal(barrier, inc=1, device_id=device, device_id_type=MESH)

    moves = (
        (x_any, xv),
        (dx_any, dxv),
        (hw_any, hwv),
        (scale_any, scale_ref),
        (shift_any, shift_ref),
        (inw_any, inwv),
        (bias_any, bias_ref),
        (inb_any, inb_ref),
        (gain_any, gain_ref),
    )
    loads = [pltpu.make_async_copy(src, dst, load_sem.at[k]) for k, (src, dst) in enumerate(moves)]
    for copy in loads:
        copy.start()

    spare = pl.multiple_of(192 - 192 * half, 64)
    midw[:, pl.ds(spare, 64), :] = jnp.zeros((27, 64, CH), BF16)
    own_rows = pl.multiple_of(half * 64 + core * SHARE, 32)
    mid_copy = pltpu.make_async_copy(mid_any, midw.at[:, pl.ds(own_rows, SHARE), :], mid_sem)

    for copy in loads[0:5]:
        copy.wait()
    mid_copy.start()
    head_partials(xv, dxv, hwv, scale_ref, shift_ref, part)

    pl.semaphore_wait(barrier, 11)
    for device in beside_z + beside_y[0:2] + beside_x:
        pl.semaphore_signal(near_sem, inc=1, device_id=device, device_id_type=MESH)

    quarter = lax.rem(y, 4)
    main_core = lax.rem(quarter, 2)
    is_main = main_core == core

    def slab_copy(k, start):
        return pltpu.make_async_remote_copy(
            src_ref=part.at[start : TOK + 16],
            dst_ref=part_in.at[k - 1, start : TOK + 16],
            send_sem=b_send.at[k - 1],
            recv_sem=b_recv.at[k - 1],
            device_id=(seq, lax.rem(slab + k, SLABS)),
            device_id_type=MESH,
        )

    for k in (2, 3, 1):
        to_main = lax.rem(slab + k, 2) == main_core

        @pl.when(to_main)
        def _():
            slab_copy(k, 0).start()

        @pl.when(jnp.logical_not(to_main))
        def _():
            slab_copy(k, 64).start()

    for copy in loads[5:]:
        copy.wait()
    for par in range(2):
        for q in range(2):
            for a in range(3):
                for i in range(4):
                    for j in range(4):
                        tap_row, tap_col = (i - par, j - q)
                        cell = (i // 2) * 8 + (j // 2) * 4 + (i % 2) * 2 + j % 2
                        rows = slice(a * 256 + cell * 16, a * 256 + cell * 16 + 16)
                        if 0 <= tap_row < 3 and 0 <= tap_col < 3:
                            piece = inwv[a * 9 + tap_row * 3 + tap_col]
                        else:
                            piece = jnp.zeros((16, CH), BF16)
                        wide[par * 2 + q, rows, :] = piece

    row = lax.broadcasted_iota(jnp.int32, (256, TOK), 0)
    token = lax.broadcasted_iota(jnp.int32, (256, TOK), 1)
    t = row & 7
    col = 2 * (((row >> 5) + 4) & 7) - 1 + ((row >> 3) & 3)
    edge_row = jnp.where(t == 0, 5, jnp.where(t == 7, 0, -1))
    main_row = jnp.where((t == 0) | (t == 7), -1, t - 1)
    src_row = jnp.where(is_main, main_row, edge_row)
    hit = (src_row >= 0) & (col >= 0) & (col < 16) & (token == src_row * 16 + col)
    pick = jnp.where(hit, 1.0, 0.0).astype(BF16)

    pl.semaphore_wait(near_sem, 6)
    for device in beside_x:
        pl.semaphore_signal(far_sem, inc=1, device_id=device, device_id_type=MESH)

    @pl.when(is_main)
    def _():
        for k in (1, 3, 2):
            slab_copy(k, 0).wait_recv()

    @pl.when(jnp.logical_not(is_main))
    def _():
        for k in (1, 3, 2):
            slab_copy(k, 64).wait_recv()

    total = part[...] + part_in[0] + part_in[1] + part_in[2]
    bias = bias_ref[...].reshape(1, 64)
    patches = head_finish(total, jnp.concatenate([bias, bias], axis=1))
    spread = jnp.dot(pick, patches, preferred_element_type=F32).astype(BF16)
    tiles[...] = spread.reshape(CG, 32, 128)

    c_copies = []
    for k in (4, 3, 5, 2, 6, 1, 7):
        to = lax.rem(y + k, CG)
        c_copies.append(
            pltpu.make_async_remote_copy(
                src_ref=tiles.at[to],
                dst_ref=tiles_in.at[y],
                send_sem=c_send.at[k],
                recv_sem=c_recv.at[k],
                device_id=(group * CG + to, slab),
                device_id_type=MESH,
            )
        )
        c_copies[-1].start()
    tiles_in[y] = tiles[y]

    mid_swap = pltpu.make_async_remote_copy(
        src_ref=mid_any,
        dst_ref=midw.at[:, pl.ds(own_rows, SHARE), :],
        send_sem=m_send,
        recv_sem=m_recv,
        device_id=(seq, half * 2 + 1 - core),
        device_id_type=MESH,
    )
    mid_swap.start()

    for copy in c_copies:
        copy.wait_recv()
    t32 = lax.broadcasted_iota(jnp.int32, (32, 128), 0) & 7
    for f in range(2):
        for b in range(2):
            q = 2 * b + core
            main = tiles_in[4 * f + q].astype(F32)
            above = tiles_in[4 * f + jnp.maximum(q - 1, 0)].astype(F32)
            below = tiles_in[4 * f + jnp.minimum(q + 1, 3)].astype(F32)
            value = main
            value = value + jnp.where((t32 == 0) & (q > 0), above, 0.0)
            value = value + jnp.where((t32 == 7) & (q < 3), below, 0.0)
            block[f * 2 + b] = value.astype(BF16)

    g_copies = []
    for d in (2, 1, 0):
        g_copies.append(
            pltpu.make_async_remote_copy(
                src_ref=block,
                dst_ref=grid.at[2 - d],
                send_sem=g_send.at[d],
                recv_sem=g_recv.at[d],
                device_id=(lax.rem(group + d + late, GROUPS) * CG + y, slab),
                device_id_type=MESH,
            )
        )
    pl.semaphore_wait(far_sem, 2)
    g_copies[0].start()
    g_copies[1].start()

    @pl.when(y < 4)
    def _():
        g_copies[2].start()
        g_copies[2].wait()

    @pl.when(y >= 4)
    def _():
        grid[2] = block[...]

    g_copies[0].wait_recv()
    g_copies[1].wait_recv()

    lane = lanes_of((2, 8, 128))
    low = lane < 64
    for slot in range(3):
        keep = jnp.where(tile_group >= 2 - slot, 1.0, 0.0)
        for f in range(2):
            cols = []
            turned = []
            cell = grid[slot, 2 * f : 2 * f + 2].astype(F32).reshape(2, 4, 8, 128) * keep
            for w in range(4):
                value = cell[:, w]
                cols.append(value)
                turned.append(pltpu.roll(value, 64, 2))
            for kind in range(2):
                for w in range(3):
                    if kind == 0:
                        pair = jnp.where(low, cols[w], turned[w + 1])
                    else:
                        pair = jnp.where(low, turned[w], cols[w + 1])
                    below = pltpu.roll(pair, 7, 1)
                    base = (slot * 2 + f) * 96 + kind * 48 + w * 16
                    pairs[base : base + 16, 0:128] = pair.reshape(16, 128).astype(BF16)
                    pairs[base : base + 16, 128:256] = below.reshape(16, 128).astype(BF16)

    window = jnp.concatenate([pairs[0:384], pairs[96:480], pairs[192:576]], axis=1)
    bias_in = inb_ref[...].reshape(1, 1, CH)
    gain = gain_ref[...].reshape(1, 1, CH)
    first_half = half == 0
    gain_own = jnp.where(first_half, gain[..., 0:256], gain[..., 128:384])
    shape = (4, 48, 1)
    frame = lax.broadcasted_iota(jnp.int32, shape, 0)
    line = lax.broadcasted_iota(jnp.int32, shape, 1)
    s = line & 7
    b_of = (line >> 3) & 1
    w_of = line >> 4
    for par in range(2):
        for q in range(2):
            conv = jnp.dot(window, wide[par * 2 + q], preferred_element_type=F32)
            conv = conv.reshape(4, 2, 48, CH)
            feat = conv[:, 0] + bias_in
            dfeat = conv[:, 1]
            scale_inv = lax.rsqrt(jnp.mean(feat * feat, axis=-1, keepdims=True) + 1e-06)
            along = jnp.mean(feat * dfeat, axis=-1, keepdims=True)
            feat_own = jnp.where(first_half, feat[..., 0:256], feat[..., 128:384])
            dfeat_own = jnp.where(first_half, dfeat[..., 0:256], dfeat[..., 128:384])
            normed = gain_own * feat_own * scale_inv
            tang = gain_own * scale_inv * (dfeat_own - feat_own * (scale_inv * scale_inv * along))
            sig = 1.0 / (1.0 + jnp.exp(-normed))
            act = sig * (1.0 + normed * (1.0 - sig)) * tang
            out_side = (frame < 2) & (tile_group == 0)
            if q == 0:
                out_side = out_side | ((w_of == 0) & (column == 0))
            else:
                out_side = out_side | ((w_of == 2) & (column == CG - 1))
            if par == 0:
                out_side = out_side | ((s == 0) & (2 * b_of + core == 0))
            else:
                out_side = out_side | ((s == 6) & (2 * b_of + core == 3))
            act = jnp.where(out_side, 0.0, act)
            moved = pltpu.roll(act.reshape(24, 8, 256), 7, 1).reshape(4, 3, 2, 8, 256)
            act = act.reshape(4, 3, 2, 8, 256)
            for plane, value in ((par, act), (par + 2, moved)):
                for a in range(3):
                    both = jnp.concatenate([value[a], value[a + 1]], axis=2).astype(BF16)
                    for w in range(3):
                        acts[:, plane, 2 * w + q, a] = both[w]
            keep = dfeat[2:4].reshape(2, 3, 2, 8, CH)
            keep = jnp.where(first_half, keep[:, :, 0], keep[:, :, 1])
            if par == 0:
                keep = pltpu.roll(keep.reshape(6, 8, CH), 7, 1).reshape(2, 3, 8, CH)
            for w in range(3):
                place = 2 * w + q - 1
                if 0 <= place < 4:
                    resid[1 - par, place] = keep[:, w]

    mid_copy.wait()
    mid_swap.wait()

    row = lax.broadcasted_iota(jnp.int32, (TOK, 128), 0)
    src = lax.broadcasted_iota(jnp.int32, (TOK, 128), 1)
    upper = row >= 48
    inner = jnp.where(upper, row - 48, row)
    want = ((inner >> 2) & 1) * 64 + (inner & 3) * 16 + jnp.where(upper, 8, 0) + (inner >> 3)
    order = jnp.where(src == want, 1.0, 0.0).astype(BF16)

    def mid_conv(block_of):
        acc = jnp.zeros((128, CH), F32)
        for a in range(3):
            for b in range(3):
                for c in range(3):
                    taken = acts[block_of, b : b + 2, c : c + 4, a].reshape(128, 256)
                    acc = acc + jnp.dot(taken, midw[a * 9 + b * 3 + c], preferred_element_type=F32)
        return acc

    other = mid_conv(1 - half).astype(BF16)
    sums_out[...] = jnp.dot(order, other, preferred_element_type=F32).astype(BF16)
    swap = pltpu.make_async_remote_copy(
        src_ref=sums_out,
        dst_ref=sums_in,
        send_sem=r_send,
        recv_sem=r_recv,
        device_id=(seq, (1 - half) * 2 + core),
        device_id_type=MESH,
    )
    swap.start()
    mine = mid_conv(half) + resid[...].reshape(128, CH)
    high = mine.astype(BF16)
    low_part = (mine - high.astype(F32)).astype(BF16)
    mine = jnp.dot(order, high, preferred_element_type=F32) + jnp.dot(order, low_part, preferred_element_type=F32)
    swap.wait_recv()
    out_ref[...] = (mine + sums_in[...].astype(F32)).astype(BF16)

    for k in (1, 2, 3):
        to_main = lax.rem(slab + k, 2) == main_core

        @pl.when(to_main)
        def _():
            slab_copy(k, 0).wait_send()

        @pl.when(jnp.logical_not(to_main))
        def _():
            slab_copy(k, 64).wait_send()

    for copy in c_copies + g_copies[0:2]:
        copy.wait_send()
    swap.wait_send()


def shards(hidden, tangent, mod_shift, mod_scale, head_weight, head_bias, in_weight, in_bias, norm_gain, mid_weight):
    any_spec = pl.BlockSpec(memory_space=pl.ANY)
    vmem = pl.BlockSpec(memory_space=pltpu.VMEM)
    dma = pltpu.SemaphoreType.DMA
    out = pl.pallas_call(
        kernel,
        out_shape=jax.ShapeDtypeStruct((TOK, CH), BF16),
        in_specs=[any_spec] * 10,
        out_specs=vmem,
        scratch_shapes=[
            pltpu.VMEM((TOK, DS), BF16),
            pltpu.VMEM((TOK, DS), BF16),
            pltpu.VMEM((64, DS), BF16),
            pltpu.VMEM((27, 16, CH), BF16),
            pltpu.VMEM((DS,), F32),
            pltpu.VMEM((DS,), F32),
            pltpu.VMEM((64,), F32),
            pltpu.VMEM((CH,), F32),
            pltpu.VMEM((CH,), F32),
            pltpu.VMEM((TOK + 16, 128), F32),
            pltpu.VMEM((3, TOK + 16, 128), F32),
            pltpu.VMEM((CG, 32, 128), BF16),
            pltpu.VMEM((CG, 32, 128), BF16),
            pltpu.VMEM((4, 32, 128), BF16),
            pltpu.VMEM((3, 4, 32, 128), BF16),
            pltpu.VMEM((576, 256), BF16),
            pltpu.VMEM((4, 768, CH), BF16),
            pltpu.VMEM((2, 4, 6, 3, 16, 256), BF16),
            pltpu.VMEM((2, 4, 2, 8, CH), F32),
            pltpu.VMEM((27, 256, CH), BF16),
            pltpu.VMEM((TOK, CH), BF16),
            pltpu.VMEM((TOK, CH), BF16),
            pltpu.SemaphoreType.REGULAR,
            pltpu.SemaphoreType.REGULAR,
            dma((9,)),
            dma,
            dma((3,)),
            dma((3,)),
            dma((CG,)),
            dma((CG,)),
            dma((3,)),
            dma((3,)),
            dma,
            dma,
            dma,
            dma,
        ],
        compiler_params=pltpu.CompilerParams(collective_id=0, has_side_effects=True),
        name="decode",
    )(
        hidden,
        tangent,
        mod_shift,
        mod_scale,
        head_weight,
        head_bias,
        in_weight.reshape(27, 16, CH),
        in_bias,
        norm_gain,
        mid_weight.reshape(27, SHARE, CH),
    )
    return out.reshape(1, 2, 12, 4, CH)


def solution(mesh):
    return jax.shard_map(
        shards,
        mesh=mesh,
        in_specs=(
            P("seq", "slab"),
            P("seq", "slab"),
            P("slab"),
            P("slab"),
            P(None, "slab"),
            P(),
            P(),
            P(),
            P(),
            P(None, None, None, "slab", None),
        ),
        out_specs=P("seq", None, "slab", None, None),
        check_vma=False,
    )
```

```python
import jax
import jax.numpy as jnp
from jax import lax
from jax.experimental import pallas as pl
from jax.experimental.pallas import tpu as pltpu
from jax.sharding import PartitionSpec as P

D = 5120
CH = 384
CG = 8
GROUPS = 16
SLABS = 4
TOK = 96
DS = D // SLABS
SHARE = CH // SLABS
F32 = jnp.float32
BF16 = jnp.bfloat16
MESH = pl.DeviceIdType.MESH
NT = (((1,), (1,)), ((), ()))


def lanes_of(shape):
    return lax.broadcasted_iota(jnp.int32, shape, len(shape) - 1)


def head_partials(xv, dxv, hwv, scale_ref, shift_ref, part, sums):
    x = xv[...]
    dx = dxv[...]
    xf = x.astype(F32)
    dxf = dx.astype(F32)
    values = [
        jnp.sum(xf, axis=1, keepdims=True),
        jnp.sum(xf * xf, axis=1, keepdims=True),
        jnp.sum(dxf, axis=1, keepdims=True),
        jnp.sum(xf * dxf, axis=1, keepdims=True),
    ]
    lane = lanes_of((TOK, 128))
    moments = jnp.zeros((TOK, 128), F32)
    for k, value in enumerate(values):
        moments = jnp.where(lane == k, value, moments)
    moments = jnp.concatenate([moments, jnp.zeros((128 - TOK, 128), F32)], axis=0)
    w = hwv[...]
    wf = w.astype(F32) * (1.0 + scale_ref[...].reshape(1, DS))
    hi = wf.astype(BF16)
    lo = (wf - hi.astype(F32)).astype(BF16)
    shift = shift_ref[...].reshape(1, DS)
    shift_hi = shift.astype(BF16).astype(F32)
    shift_mid = (shift - shift_hi).astype(BF16).astype(F32)
    shift_lo = shift - shift_hi - shift_mid
    row = lax.broadcasted_iota(jnp.int32, (16, DS), 0)
    extra = jnp.where(row == 0, 1.0, 0.0)
    extra = jnp.where(row == 1, shift_hi, extra)
    extra = jnp.where(row == 2, shift_mid, extra)
    extra = jnp.where(row == 3, shift_lo, extra).astype(BF16)
    both = jnp.concatenate([x, dx, extra], axis=0)
    split = jnp.concatenate([hi, lo], axis=0)
    prod = lax.dot_general(both, split, NT, preferred_element_type=F32)
    prod = prod + pltpu.roll(prod, 64, 1)
    twice = jnp.concatenate([w, w], axis=0)
    shifted = lax.dot_general(extra, twice, NT, preferred_element_type=F32)
    weight_sum = prod[2 * TOK : 2 * TOK + 1]
    shift_sum = shifted[1:2] + shifted[2:3] + shifted[3:4]
    value = jnp.where(lane < 64, prod[0:TOK], prod[TOK : 2 * TOK])
    value = value - jnp.where(lane < 64, values[0] / DS, values[2] / DS) * weight_sum
    send = value.astype(BF16)
    part[0:64, :] = send[16:80]
    part[64:80, :] = send[0:16]
    part[80:96, :] = send[80:96]
    const = jnp.where(lanes_of((1, 128)) < 64, weight_sum, shift_sum)
    row8 = lax.broadcasted_iota(jnp.int32, (8, 128), 0)
    sums[...] = jnp.where(row8 == 4, const, jnp.transpose(moments)[0:8])
    return value


def head_finish(own, part_in, sums, bias):
    moments = jnp.concatenate([sums, jnp.zeros((96, 128), F32)], axis=0)
    moments = jnp.transpose(moments)[0:TOK]
    total = moments[:, 0:8] + moments[:, 8:16] + moments[:, 16:24] + moments[:, 24:32]
    lane = lanes_of((TOK, 128))
    lane1 = lanes_of((8, 128))
    mean = total[:, 0:1] / D
    mean_tangent = total[:, 2:3] / D
    received = part_in[0].astype(F32) + part_in[1].astype(F32) + part_in[2].astype(F32)
    part = own + jnp.concatenate([received[64:80], received[0:64], received[80:96]], axis=0)
    shift_term = jnp.zeros((1, 128), F32)
    for k in range(4):
        const = jnp.broadcast_to(sums[8 * k + 4 : 8 * k + 5], (8, 128))
        turned = pltpu.roll(const, 64, 1)
        weight_sum = jnp.where(lane1 < 64, const, turned)[0:1]
        shift_term = shift_term + turned[0:1]
        off = moments[:, 8 * k : 8 * k + 1] / DS - mean
        off_tangent = moments[:, 8 * k + 2 : 8 * k + 3] / DS - mean_tangent
        part = part + jnp.where(lane < 64, off, off_tangent) * weight_sum
    variance = total[:, 1:2] / D - mean * mean
    inverse = lax.rsqrt(variance + 1e-06)
    project = inverse * (total[:, 3:4] / D - mean * mean_tangent)
    value = inverse * part
    primal = value + shift_term + bias
    tangent = value - inverse * project * pltpu.roll(value, 64, 1)
    return jnp.where(lane < 64, primal, tangent).astype(BF16)


def kernel(
    x_any, dx_any, shift_any, scale_any, hw_any, bias_any, inw_any, inb_any, gain_any, mid_any,
    out_ref,
    xv, dxv, hwv, inwv, shift_ref, scale_ref, bias_ref, inb_ref, gain_ref, part, part_in, sums, sums_row_in, tiles, tiles_in, block, grid, pairs, wide, acts, resid,
    midw, sums_out, sums_in,
    near_sem, far_sem, load_sem, mid_sem, b_send, b_recv, x_send, x_recv, c_send, c_recv, g_send, g_recv, m_send, m_recv, r_send, r_recv,
):
    seq = lax.axis_index("seq")
    slab = lax.axis_index("slab")
    y = lax.rem(seq, CG)
    group = lax.div(seq, CG)
    core = lax.rem(slab, 2)
    half = lax.div(slab, 2)
    late = (y < 4).astype(jnp.int32)
    tile_group = lax.rem(group - late + GROUPS, GROUPS)
    column = lax.rem(y + 4, CG)

    part_in[:, 0:64, :] = jnp.zeros((3, 64, 128), BF16)
    barrier = pltpu.get_barrier_semaphore()
    z_hi = lax.div(group, 4)
    x = lax.rem(group, 4)

    def place(z_to, x_to, y_to):
        return (lax.rem(z_to, 4) * 4 + lax.rem(x_to, 4)) * CG + lax.rem(y_to, CG)

    beside_x = [(place(z_hi, x + k, y), slab) for k in (1, 3)]
    beside_z = [(place(z_hi + k, x, y), slab) for k in (1, 3)]
    beside_y = [(place(z_hi, x, y + k), slab) for k in (2, 6, 1, 7)]
    in_slab = [(seq, lax.rem(slab + k, SLABS)) for k in range(1, SLABS)]
    for device in beside_z + beside_y + beside_x + in_slab:
        pl.semaphore_signal(barrier, inc=1, device_id=device, device_id_type=MESH)

    moves = (
        (x_any.at[0:48], xv.at[0:48]),
        (x_any.at[48:96], xv.at[48:96]),
        (dx_any.at[0:48], dxv.at[0:48]),
        (dx_any.at[48:96], dxv.at[48:96]),
        (hw_any, hwv),
        (scale_any, scale_ref),
        (shift_any, shift_ref),
        (inw_any, inwv),
        (bias_any, bias_ref),
        (inb_any, inb_ref),
        (gain_any, gain_ref),
    )
    loads = [pltpu.make_async_copy(src, dst, load_sem.at[k]) for k, (src, dst) in enumerate(moves)]
    for copy in loads[0:7]:
        copy.start()

    spare = pl.multiple_of(192 - 192 * half, 64)
    midw[:, pl.ds(spare, 64), :] = jnp.zeros((27, 64, CH), BF16)
    own_rows = pl.multiple_of(half * 64 + core * SHARE, 32)
    mid_copy = pltpu.make_async_copy(mid_any, midw.at[:, pl.ds(own_rows, SHARE), :], mid_sem)

    pl.semaphore_wait(barrier, 11)
    for device in beside_z + beside_y[0:2] + beside_x:
        pl.semaphore_signal(near_sem, inc=1, device_id=device, device_id_type=MESH)

    for copy in loads[0:7]:
        copy.wait()
    for copy in loads[7:]:
        copy.start()
    mid_copy.start()
    own = head_partials(xv, dxv, hwv, scale_ref, shift_ref, part, sums)

    quarter = lax.rem(y, 4)
    main_core = lax.rem(quarter, 2)
    is_main = main_core == core

    def slab_copy(k, start):
        return pltpu.make_async_remote_copy(
            src_ref=part.at[start:TOK],
            dst_ref=part_in.at[k - 1, start:TOK],
            send_sem=b_send.at[k - 1],
            recv_sem=b_recv.at[k - 1],
            device_id=(seq, lax.rem(slab + k, SLABS)),
            device_id_type=MESH,
        )

    sum_copies = []
    for k in (2, 3, 1):
        to_main = lax.rem(slab + k, 2) == main_core
        sum_copies.append(
            pltpu.make_async_remote_copy(
                src_ref=sums,
                dst_ref=sums_row_in.at[k - 1],
                send_sem=x_send.at[k - 1],
                recv_sem=x_recv.at[k - 1],
                device_id=(seq, lax.rem(slab + k, SLABS)),
                device_id_type=MESH,
            )
        )
        sum_copies[-1].start()

        @pl.when(to_main)
        def _():
            slab_copy(k, 0).start()

        @pl.when(jnp.logical_not(to_main))
        def _():
            slab_copy(k, 64).start()

    row = lax.broadcasted_iota(jnp.int32, (256, TOK), 0)
    token = lax.broadcasted_iota(jnp.int32, (256, TOK), 1)
    line = row & 31
    t = line & 7
    main_row = jnp.where((t == 0) | (t == 7), -1, t - 1)
    edge_row = jnp.where(line < 8, jnp.where((line & 1) == 0, 5, 0), -1)
    src_row = jnp.where(is_main, main_row, edge_row)
    col = 2 * (((row >> 5) + 4) & 7) - 1 + jnp.where(is_main, line >> 3, line >> 1)
    hit = (src_row >= 0) & (col >= 0) & (col < 16) & (token == src_row * 16 + col)
    pick = jnp.where(hit, 1.0, 0.0).astype(BF16)

    @pl.when(is_main)
    def _():
        for k in (1, 3, 2):
            slab_copy(k, 0).wait_recv()

    @pl.when(jnp.logical_not(is_main))
    def _():
        for k in (1, 3, 2):
            slab_copy(k, 64).wait_recv()

    for copy in sum_copies:
        copy.wait_recv()
    all_sums = jnp.concatenate([sums[...], sums_row_in[0], sums_row_in[1], sums_row_in[2]], axis=0)
    loads[8].wait()
    bias = bias_ref[...].reshape(1, 64)
    patches = head_finish(own, part_in, all_sums, jnp.concatenate([bias, bias], axis=1))
    spread = jnp.dot(pick, patches, preferred_element_type=F32).astype(BF16)
    tiles[...] = spread.reshape(CG, 32, 128)

    pl.semaphore_wait(near_sem, 6)
    for device in beside_x:
        pl.semaphore_signal(far_sem, inc=1, device_id=device, device_id_type=MESH)

    def y_copy(k, rows):
        to = lax.rem(y + k, CG)
        return pltpu.make_async_remote_copy(
            src_ref=tiles.at[to, 0:rows],
            dst_ref=tiles_in.at[y, 0:rows],
            send_sem=c_send.at[k],
            recv_sem=c_recv.at[k],
            device_id=(group * CG + to, slab),
            device_id_type=MESH,
        )

    steps = (4, 3, 5, 2, 6, 1, 7)

    @pl.when(is_main)
    def _():
        for k in steps:
            y_copy(k, 32).start()

    @pl.when(jnp.logical_not(is_main))
    def _():
        for k in steps:
            y_copy(k, 8).start()

    tiles_in[y] = tiles[y]

    for copy in (loads[7], loads[9], loads[10]):
        copy.wait()
    for par in range(2):
        for q in range(2):
            for a in range(3):
                for i in range(4):
                    for j in range(4):
                        tap_row, tap_col = (i - par, j - q)
                        cell = (i // 2) * 8 + (j // 2) * 4 + (i % 2) * 2 + j % 2
                        rows = slice(a * 256 + cell * 16, a * 256 + cell * 16 + 16)
                        if 0 <= tap_row < 3 and 0 <= tap_col < 3:
                            piece = inwv[a * 9 + tap_row * 3 + tap_col]
                        else:
                            piece = jnp.zeros((16, CH), BF16)
                        wide[par * 2 + q, rows, :] = piece

    @pl.when(is_main)
    def _():
        for k in steps:
            y_copy(k, 8 if k % 2 else 32).wait_recv()

    @pl.when(jnp.logical_not(is_main))
    def _():
        for k in steps:
            y_copy(k, 32 if k % 2 else 8).wait_recv()

    to_row = lax.broadcasted_iota(jnp.int32, (32, 48), 0)
    from_row = lax.broadcasted_iota(jnp.int32, (32, 48), 1)
    col2 = (to_row >> 3) * 2
    t = to_row & 7
    for b in range(2):
        q = 2 * b + core
        joined = (to_row == from_row) | ((t == 0) & (from_row == 32 + col2) & (q > 0))
        joined = joined | ((t == 7) & (from_row == 41 + col2) & (q < 3))
        join = jnp.where(joined, 1.0, 0.0).astype(BF16)
        for f in range(2):
            main = tiles_in[4 * f + q].astype(F32)
            above = tiles_in[4 * f + jnp.maximum(q - 1, 0), 0:8].astype(F32)
            below = tiles_in[4 * f + jnp.minimum(q + 1, 3), 0:8].astype(F32)
            value = jnp.concatenate([main, above, below], axis=0).astype(BF16)
            block[f * 2 + b] = jnp.dot(join, value, preferred_element_type=F32).astype(BF16)

    g_copies = []
    for d in (2, 1, 0):
        g_copies.append(
            pltpu.make_async_remote_copy(
                src_ref=block,
                dst_ref=grid.at[2 - d],
                send_sem=g_send.at[d],
                recv_sem=g_recv.at[d],
                device_id=(lax.rem(group + d + late, GROUPS) * CG + y, slab),
                device_id_type=MESH,
            )
        )
    pl.semaphore_wait(far_sem, 2)
    g_copies[0].start()
    g_copies[1].start()

    @pl.when(y < 4)
    def _():
        g_copies[2].start()

    @pl.when(y >= 4)
    def _():
        grid[2] = block[...]

    mid_swap = pltpu.make_async_remote_copy(
        src_ref=mid_any,
        dst_ref=midw.at[:, pl.ds(own_rows, SHARE), :],
        send_sem=m_send,
        recv_sem=m_recv,
        device_id=(seq, half * 2 + 1 - core),
        device_id_type=MESH,
    )
    mid_swap.start()

    g_copies[0].wait_recv()
    g_copies[1].wait_recv()

    @pl.when(y < 4)
    def _():
        g_copies[2].wait()


    lane = lanes_of((2, 8, 128))
    low = lane < 64
    for slot in range(3):
        keep = jnp.where(tile_group >= 2 - slot, 1.0, 0.0)
        for f in range(2):
            cols = []
            turned = []
            cell = grid[slot, 2 * f : 2 * f + 2].astype(F32).reshape(2, 4, 8, 128) * keep
            for w in range(4):
                value = cell[:, w]
                cols.append(value)
                turned.append(pltpu.roll(value, 64, 2))
            for kind in range(2):
                for w in range(3):
                    if kind == 0:
                        pair = jnp.where(low, cols[w], turned[w + 1])
                    else:
                        pair = jnp.where(low, turned[w], cols[w + 1])
                    below = pltpu.roll(pair, 7, 1)
                    base = (slot * 2 + f) * 96 + kind * 48 + w * 16
                    pairs[base : base + 16, 0:128] = pair.reshape(16, 128).astype(BF16)
                    pairs[base : base + 16, 128:256] = below.reshape(16, 128).astype(BF16)

    window = jnp.concatenate([pairs[0:384], pairs[96:480], pairs[192:576]], axis=1)
    bias_in = inb_ref[...].reshape(1, 1, CH)
    gain = gain_ref[...].reshape(1, 1, CH)
    first_half = half == 0
    gain_own = jnp.where(first_half, gain[..., 0:256], gain[..., 128:384])
    shape = (4, 48, 1)
    frame = lax.broadcasted_iota(jnp.int32, shape, 0)
    line = lax.broadcasted_iota(jnp.int32, shape, 1)
    s = line & 7
    b_of = (line >> 3) & 1
    w_of = line >> 4
    for par in range(2):
        for q in range(2):
            conv = jnp.dot(window, wide[par * 2 + q], preferred_element_type=F32)
            conv = conv.reshape(4, 2, 48, CH)
            feat = conv[:, 0] + bias_in
            dfeat = conv[:, 1]
            scale_inv = lax.rsqrt(jnp.mean(feat * feat, axis=-1, keepdims=True) + 1e-06)
            along = jnp.mean(feat * dfeat, axis=-1, keepdims=True)
            feat_own = jnp.where(first_half, feat[..., 0:256], feat[..., 128:384])
            dfeat_own = jnp.where(first_half, dfeat[..., 0:256], dfeat[..., 128:384])
            normed = gain_own * feat_own * scale_inv
            tang = gain_own * scale_inv * (dfeat_own - feat_own * (scale_inv * scale_inv * along))
            sig = 1.0 / (1.0 + jnp.exp(-normed))
            act = sig * (1.0 + normed * (1.0 - sig)) * tang
            out_side = (frame < 2) & (tile_group == 0)
            if q == 0:
                out_side = out_side | ((w_of == 0) & (column == 0))
            else:
                out_side = out_side | ((w_of == 2) & (column == CG - 1))
            if par == 0:
                out_side = out_side | ((s == 0) & (2 * b_of + core == 0))
            else:
                out_side = out_side | ((s == 6) & (2 * b_of + core == 3))
            act = jnp.where(out_side, 0.0, act)
            moved = pltpu.roll(act.reshape(24, 8, 256), 7, 1).reshape(4, 3, 2, 8, 256)
            act = act.reshape(4, 3, 2, 8, 256)
            for plane, value in ((par, act), (par + 2, moved)):
                for a in range(3):
                    both = jnp.concatenate([value[a], value[a + 1]], axis=2).astype(BF16)
                    for w in range(3):
                        acts[:, plane, 2 * w + q, a] = both[w]
            keep = dfeat[2:4].reshape(2, 3, 2, 8, CH)
            keep = jnp.where(first_half, keep[:, :, 0], keep[:, :, 1])
            if par == 0:
                keep = pltpu.roll(keep.reshape(6, 8, CH), 7, 1).reshape(2, 3, 8, CH)
            for w in range(3):
                place = 2 * w + q - 1
                if 0 <= place < 4:
                    resid[1 - par, place] = keep[:, w]

    mid_copy.wait()
    mid_swap.wait()

    row = lax.broadcasted_iota(jnp.int32, (TOK, 128), 0)
    src = lax.broadcasted_iota(jnp.int32, (TOK, 128), 1)
    upper = row >= 48
    inner = jnp.where(upper, row - 48, row)
    want = ((inner >> 2) & 1) * 64 + (inner & 3) * 16 + jnp.where(upper, 8, 0) + (inner >> 3)
    order = jnp.where(src == want, 1.0, 0.0).astype(BF16)

    def mid_conv(block_of, lanes):
        acc = jnp.zeros((128, lanes.stop - lanes.start), F32)
        for a in range(3):
            for b in range(3):
                for c in range(3):
                    taken = acts[block_of, b : b + 2, c : c + 4, a].reshape(128, 256)
                    weight = midw[a * 9 + b * 3 + c, :, lanes]
                    acc = acc + jnp.dot(taken, weight, preferred_element_type=F32)
        return acc

    swaps = []
    for n, lanes in enumerate((slice(0, CH),)):
        other = mid_conv(1 - half, lanes).astype(BF16)
        sums_out[:, lanes] = jnp.dot(order, other, preferred_element_type=F32).astype(BF16)
        swaps.append(
            pltpu.make_async_remote_copy(
                src_ref=sums_out.at[:, lanes],
                dst_ref=sums_in.at[:, lanes],
                send_sem=r_send.at[n],
                recv_sem=r_recv.at[n],
                device_id=(seq, (1 - half) * 2 + core),
                device_id_type=MESH,
            )
        )
        swaps[-1].start()
    mine = mid_conv(half, slice(0, CH)) + resid[...].reshape(128, CH)
    high = mine.astype(BF16)
    low_part = (mine - high.astype(F32)).astype(BF16)
    mine = jnp.dot(order, high, preferred_element_type=F32) + jnp.dot(order, low_part, preferred_element_type=F32)
    for copy in swaps:
        copy.wait_recv()
    out_ref[...] = (mine + sums_in[...].astype(F32)).astype(BF16)

    for k in (1, 2, 3):
        to_main = lax.rem(slab + k, 2) == main_core

        @pl.when(to_main)
        def _():
            slab_copy(k, 0).wait_send()

        @pl.when(jnp.logical_not(to_main))
        def _():
            slab_copy(k, 64).wait_send()

    @pl.when(is_main)
    def _():
        for k in steps:
            y_copy(k, 32).wait_send()

    @pl.when(jnp.logical_not(is_main))
    def _():
        for k in steps:
            y_copy(k, 8).wait_send()

    for copy in sum_copies + g_copies[0:2]:
        copy.wait_send()
    for copy in swaps:
        copy.wait_send()


def shards(hidden, tangent, mod_shift, mod_scale, head_weight, head_bias, in_weight, in_bias, norm_gain, mid_weight):
    any_spec = pl.BlockSpec(memory_space=pl.ANY)
    dma = pltpu.SemaphoreType.DMA
    out = pl.pallas_call(
        kernel,
        out_shape=jax.ShapeDtypeStruct((TOK, CH), BF16),
        in_specs=[any_spec] * 10,
        out_specs=pl.BlockSpec(memory_space=pltpu.VMEM),
        scratch_shapes=[
            pltpu.VMEM((TOK, DS), BF16),
            pltpu.VMEM((TOK, DS), BF16),
            pltpu.VMEM((64, DS), BF16),
            pltpu.VMEM((27, 16, CH), BF16),
            pltpu.VMEM((DS,), F32),
            pltpu.VMEM((DS,), F32),
            pltpu.VMEM((64,), F32),
            pltpu.VMEM((CH,), F32),
            pltpu.VMEM((CH,), F32),
            pltpu.VMEM((TOK, 128), BF16),
            pltpu.VMEM((3, TOK, 128), BF16),
            pltpu.VMEM((8, 128), F32),
            pltpu.VMEM((3, 8, 128), F32),
            pltpu.VMEM((CG, 32, 128), BF16),
            pltpu.VMEM((CG, 32, 128), BF16),
            pltpu.VMEM((4, 32, 128), BF16),
            pltpu.VMEM((3, 4, 32, 128), BF16),
            pltpu.VMEM((576, 256), BF16),
            pltpu.VMEM((4, 768, CH), BF16),
            pltpu.VMEM((2, 4, 6, 3, 16, 256), BF16),
            pltpu.VMEM((2, 4, 2, 8, CH), F32),
            pltpu.VMEM((27, 256, CH), BF16),
            pltpu.VMEM((TOK, CH), BF16),
            pltpu.VMEM((TOK, CH), BF16),
            pltpu.SemaphoreType.REGULAR,
            pltpu.SemaphoreType.REGULAR,
            dma((11,)),
            dma,
            dma((3,)),
            dma((3,)),
            dma((3,)),
            dma((3,)),
            dma((CG,)),
            dma((CG,)),
            dma((3,)),
            dma((3,)),
            dma,
            dma,
            dma((1,)),
            dma((1,)),
        ],
        compiler_params=pltpu.CompilerParams(collective_id=0, has_side_effects=True),
        name="decode",
    )(
        hidden,
        tangent,
        mod_shift,
        mod_scale,
        head_weight,
        head_bias,
        in_weight.reshape(27, 16, CH),
        in_bias,
        norm_gain,
        mid_weight.reshape(27, SHARE, CH),
    )
    return out.reshape(1, 2, 12, 4, CH)


def solution(mesh):
    return jax.shard_map(
        shards,
        mesh=mesh,
        in_specs=(
            P("seq", "slab"),
            P("seq", "slab"),
            P("slab"),
            P("slab"),
            P(None, "slab"),
            P(),
            P(),
            P(),
            P(),
            P(None, None, None, "slab", None),
        ),
        out_specs=P("seq", None, "slab", None, None),
        check_vma=False,
    )
```

```python
import jax
import jax.numpy as jnp
from jax import lax
from jax.experimental import pallas as pl
from jax.experimental.pallas import tpu as pltpu
from jax.sharding import PartitionSpec as P

D = 5120
CH = 384
CG = 8
GROUPS = 16
SLABS = 4
TOK = 96
DS = D // SLABS
SHARE = CH // SLABS
F32 = jnp.float32
BF16 = jnp.bfloat16
MESH = pl.DeviceIdType.MESH
NT = (((1,), (1,)), ((), ()))


def lanes_of(shape):
    return lax.broadcasted_iota(jnp.int32, shape, len(shape) - 1)


def head_partials(xv, dxv, hwv, scale_ref, shift_ref, part, sums):
    x = xv[...]
    dx = dxv[...]
    xf = x.astype(F32)
    dxf = dx.astype(F32)
    values = [
        jnp.sum(xf, axis=1, keepdims=True),
        jnp.sum(xf * xf, axis=1, keepdims=True),
        jnp.sum(dxf, axis=1, keepdims=True),
        jnp.sum(xf * dxf, axis=1, keepdims=True),
    ]
    lane = lanes_of((TOK, 128))
    moments = jnp.zeros((TOK, 128), F32)
    for k, value in enumerate(values):
        moments = jnp.where(lane == k, value, moments)
    moments = jnp.concatenate([moments, jnp.zeros((128 - TOK, 128), F32)], axis=0)
    w = hwv[...]
    wf = w.astype(F32) * (1.0 + scale_ref[...].reshape(1, DS))
    hi = wf.astype(BF16)
    lo = (wf - hi.astype(F32)).astype(BF16)
    shift = shift_ref[...].reshape(1, DS)
    shift_hi = shift.astype(BF16).astype(F32)
    shift_mid = (shift - shift_hi).astype(BF16).astype(F32)
    shift_lo = shift - shift_hi - shift_mid
    row = lax.broadcasted_iota(jnp.int32, (16, DS), 0)
    extra = jnp.where(row == 0, 1.0, 0.0)
    extra = jnp.where(row == 1, shift_hi, extra)
    extra = jnp.where(row == 2, shift_mid, extra)
    extra = jnp.where(row == 3, shift_lo, extra).astype(BF16)
    both = jnp.concatenate([x, dx, extra], axis=0)
    split = jnp.concatenate([hi, lo], axis=0)
    prod = lax.dot_general(both, split, NT, preferred_element_type=F32)
    prod = prod + pltpu.roll(prod, 64, 1)
    twice = jnp.concatenate([w, w], axis=0)
    shifted = lax.dot_general(extra, twice, NT, preferred_element_type=F32)
    weight_sum = prod[2 * TOK : 2 * TOK + 1]
    shift_sum = shifted[1:2] + shifted[2:3] + shifted[3:4]
    value = jnp.where(lane < 64, prod[0:TOK], prod[TOK : 2 * TOK])
    value = value - jnp.where(lane < 64, values[0] / DS, values[2] / DS) * weight_sum
    send = value.astype(BF16)
    part[0:64, :] = send[16:80]
    part[64:80, :] = send[0:16]
    part[80:96, :] = send[80:96]
    const = jnp.where(lanes_of((1, 128)) < 64, weight_sum, shift_sum)
    row8 = lax.broadcasted_iota(jnp.int32, (8, 128), 0)
    sums[...] = jnp.where(row8 == 4, const, jnp.transpose(moments)[0:8])
    return value


def head_finish(own, part_in, sums, bias):
    moments = jnp.concatenate([sums, jnp.zeros((96, 128), F32)], axis=0)
    moments = jnp.transpose(moments)[0:TOK]
    total = moments[:, 0:8] + moments[:, 8:16] + moments[:, 16:24] + moments[:, 24:32]
    lane = lanes_of((TOK, 128))
    lane1 = lanes_of((8, 128))
    mean = total[:, 0:1] / D
    mean_tangent = total[:, 2:3] / D
    received = part_in[0].astype(F32) + part_in[1].astype(F32) + part_in[2].astype(F32)
    part = own + jnp.concatenate([received[64:80], received[0:64], received[80:96]], axis=0)
    shift_term = jnp.zeros((1, 128), F32)
    for k in range(4):
        const = jnp.broadcast_to(sums[8 * k + 4 : 8 * k + 5], (8, 128))
        turned = pltpu.roll(const, 64, 1)
        weight_sum = jnp.where(lane1 < 64, const, turned)[0:1]
        shift_term = shift_term + turned[0:1]
        off = moments[:, 8 * k : 8 * k + 1] / DS - mean
        off_tangent = moments[:, 8 * k + 2 : 8 * k + 3] / DS - mean_tangent
        part = part + jnp.where(lane < 64, off, off_tangent) * weight_sum
    variance = total[:, 1:2] / D - mean * mean
    inverse = lax.rsqrt(variance + 1e-06)
    project = inverse * (total[:, 3:4] / D - mean * mean_tangent)
    value = inverse * part
    primal = value + shift_term + bias
    tangent = value - inverse * project * pltpu.roll(value, 64, 1)
    return jnp.where(lane < 64, primal, tangent).astype(BF16)


def kernel(
    x_any, dx_any, shift_any, scale_any, hw_any, bias_any, inw_any, inb_any, gain_any, mid_any,
    out_ref,
    xv, dxv, hwv, inwv, shift_ref, scale_ref, bias_ref, inb_ref, gain_ref, part, part_in, sums, sums_row_in, tiles, tiles_in, block, grid, pairs, wide, acts, resid,
    midw, sums_out, sums_in,
    near_sem, far_sem, load_sem, mid_sem, b_send, b_recv, x_send, x_recv, c_send, c_recv, g_send, g_recv, m_send, m_recv, r_send, r_recv,
):
    seq = lax.axis_index("seq")
    slab = lax.axis_index("slab")
    y = lax.rem(seq, CG)
    group = lax.div(seq, CG)
    core = lax.rem(slab, 2)
    half = lax.div(slab, 2)
    late = (y < 4).astype(jnp.int32)
    tile_group = lax.rem(group - late + GROUPS, GROUPS)
    column = lax.rem(y + 4, CG)

    part_in[:, 0:64, :] = jnp.zeros((3, 64, 128), BF16)
    barrier = pltpu.get_barrier_semaphore()
    z_hi = lax.div(group, 4)
    x = lax.rem(group, 4)

    def place(z_to, x_to, y_to):
        return (lax.rem(z_to, 4) * 4 + lax.rem(x_to, 4)) * CG + lax.rem(y_to, CG)

    beside_x = [(place(z_hi, x + k, y), slab) for k in (1, 3)]
    beside_z = [(place(z_hi + k, x, y), slab) for k in (1, 3)]
    beside_y = [(place(z_hi, x, y + k), slab) for k in (2, 6, 1, 7)]
    in_slab = [(seq, lax.rem(slab + k, SLABS)) for k in range(1, SLABS)]
    for device in beside_z + beside_y + beside_x + in_slab:
        pl.semaphore_signal(barrier, inc=1, device_id=device, device_id_type=MESH)

    moves = (
        (x_any.at[0:48], xv.at[0:48]),
        (x_any.at[48:96], xv.at[48:96]),
        (dx_any.at[0:48], dxv.at[0:48]),
        (dx_any.at[48:96], dxv.at[48:96]),
        (hw_any, hwv),
        (scale_any, scale_ref),
        (shift_any, shift_ref),
        (inw_any, inwv),
        (bias_any, bias_ref),
        (inb_any, inb_ref),
        (gain_any, gain_ref),
    )
    loads = [pltpu.make_async_copy(src, dst, load_sem.at[k]) for k, (src, dst) in enumerate(moves)]
    for copy in loads[0:7]:
        copy.start()

    spare = pl.multiple_of(192 - 192 * half, 64)
    midw[:, pl.ds(spare, 64), :] = jnp.zeros((27, 64, CH), BF16)
    own_rows = pl.multiple_of(half * 64 + core * SHARE, 32)
    mid_copy = pltpu.make_async_copy(mid_any, midw.at[:, pl.ds(own_rows, SHARE), :], mid_sem)

    pl.semaphore_wait(barrier, 11)
    for device in beside_z + beside_y[0:2] + beside_x:
        pl.semaphore_signal(near_sem, inc=1, device_id=device, device_id_type=MESH)

    for copy in loads[0:7]:
        copy.wait()
    for copy in loads[7:]:
        copy.start()
    mid_copy.start()
    own = head_partials(xv, dxv, hwv, scale_ref, shift_ref, part, sums)

    quarter = lax.rem(y, 4)
    main_core = lax.rem(quarter, 2)
    is_main = main_core == core

    def slab_copy(k, start):
        return pltpu.make_async_remote_copy(
            src_ref=part.at[start:TOK],
            dst_ref=part_in.at[k - 1, start:TOK],
            send_sem=b_send.at[k - 1],
            recv_sem=b_recv.at[k - 1],
            device_id=(seq, lax.rem(slab + k, SLABS)),
            device_id_type=MESH,
        )

    sum_copies = []
    for k in (2, 3, 1):
        to_main = lax.rem(slab + k, 2) == main_core
        sum_copies.append(
            pltpu.make_async_remote_copy(
                src_ref=sums,
                dst_ref=sums_row_in.at[k - 1],
                send_sem=x_send.at[k - 1],
                recv_sem=x_recv.at[k - 1],
                device_id=(seq, lax.rem(slab + k, SLABS)),
                device_id_type=MESH,
            )
        )
        sum_copies[-1].start()

        @pl.when(to_main)
        def _():
            slab_copy(k, 0).start()

        @pl.when(jnp.logical_not(to_main))
        def _():
            slab_copy(k, 64).start()

    row = lax.broadcasted_iota(jnp.int32, (256, TOK), 0)
    token = lax.broadcasted_iota(jnp.int32, (256, TOK), 1)
    line = row & 31
    t = line & 7
    main_row = jnp.where((t == 0) | (t == 7), -1, t - 1)
    edge_row = jnp.where(line < 8, jnp.where((line & 1) == 0, 5, 0), -1)
    src_row = jnp.where(is_main, main_row, edge_row)
    col = 2 * (((row >> 5) + 4) & 7) - 1 + jnp.where(is_main, line >> 3, line >> 1)
    hit = (src_row >= 0) & (col >= 0) & (col < 16) & (token == src_row * 16 + col)
    pick = jnp.where(hit, 1.0, 0.0).astype(BF16)

    @pl.when(is_main)
    def _():
        for k in (1, 3, 2):
            slab_copy(k, 0).wait_recv()

    @pl.when(jnp.logical_not(is_main))
    def _():
        for k in (1, 3, 2):
            slab_copy(k, 64).wait_recv()

    for copy in sum_copies:
        copy.wait_recv()
    all_sums = jnp.concatenate([sums[...], sums_row_in[0], sums_row_in[1], sums_row_in[2]], axis=0)
    loads[8].wait()
    bias = bias_ref[...].reshape(1, 64)
    patches = head_finish(own, part_in, all_sums, jnp.concatenate([bias, bias], axis=1))
    spread = jnp.dot(pick, patches, preferred_element_type=F32).astype(BF16)
    tiles[...] = spread.reshape(CG, 32, 128)

    pl.semaphore_wait(near_sem, 6)
    for device in beside_x:
        pl.semaphore_signal(far_sem, inc=1, device_id=device, device_id_type=MESH)

    def y_copy(k, rows):
        to = lax.rem(y + k, CG)
        return pltpu.make_async_remote_copy(
            src_ref=tiles.at[to, 0:rows],
            dst_ref=tiles_in.at[y, 0:rows],
            send_sem=c_send.at[k],
            recv_sem=c_recv.at[k],
            device_id=(group * CG + to, slab),
            device_id_type=MESH,
        )

    steps = (4, 3, 5, 2, 6, 1, 7)

    @pl.when(is_main)
    def _():
        for k in steps:
            y_copy(k, 32).start()

    @pl.when(jnp.logical_not(is_main))
    def _():
        for k in steps:
            y_copy(k, 8).start()

    tiles_in[y] = tiles[y]

    for copy in (loads[7], loads[9], loads[10]):
        copy.wait()
    for par in range(2):
        for q in range(2):
            for a in range(3):
                for i in range(4):
                    for j in range(4):
                        tap_row, tap_col = (i - par, j - q)
                        cell = (i // 2) * 8 + (j // 2) * 4 + (i % 2) * 2 + j % 2
                        rows = slice(a * 256 + cell * 16, a * 256 + cell * 16 + 16)
                        if 0 <= tap_row < 3 and 0 <= tap_col < 3:
                            piece = inwv[a * 9 + tap_row * 3 + tap_col]
                        else:
                            piece = jnp.zeros((16, CH), BF16)
                        wide[par * 2 + q, rows, :] = piece

    @pl.when(is_main)
    def _():
        for k in steps:
            y_copy(k, 8 if k % 2 else 32).wait_recv()

    @pl.when(jnp.logical_not(is_main))
    def _():
        for k in steps:
            y_copy(k, 32 if k % 2 else 8).wait_recv()

    to_row = lax.broadcasted_iota(jnp.int32, (32, 48), 0)
    from_row = lax.broadcasted_iota(jnp.int32, (32, 48), 1)
    col2 = (to_row >> 3) * 2
    t = to_row & 7
    for b in range(2):
        q = 2 * b + core
        joined = (to_row == from_row) | ((t == 0) & (from_row == 32 + col2) & (q > 0))
        joined = joined | ((t == 7) & (from_row == 41 + col2) & (q < 3))
        join = jnp.where(joined, 1.0, 0.0).astype(BF16)
        for f in range(2):
            main = tiles_in[4 * f + q].astype(F32)
            above = tiles_in[4 * f + jnp.maximum(q - 1, 0), 0:8].astype(F32)
            below = tiles_in[4 * f + jnp.minimum(q + 1, 3), 0:8].astype(F32)
            value = jnp.concatenate([main, above, below], axis=0).astype(BF16)
            block[f * 2 + b] = jnp.dot(join, value, preferred_element_type=F32).astype(BF16)

    g_copies = []
    for d in (2, 1, 0):
        g_copies.append(
            pltpu.make_async_remote_copy(
                src_ref=block,
                dst_ref=grid.at[2 - d],
                send_sem=g_send.at[d],
                recv_sem=g_recv.at[d],
                device_id=(lax.rem(group + d + late, GROUPS) * CG + y, slab),
                device_id_type=MESH,
            )
        )
    pl.semaphore_wait(far_sem, 2)
    for copy, d in ((g_copies[0], 2), (g_copies[1], 1)):

        @pl.when(group + d < GROUPS)
        def _():
            copy.start()


    @pl.when(y < 4)
    def _():
        g_copies[2].start()

    @pl.when(y >= 4)
    def _():
        grid[2] = block[...]

    mid_swap = pltpu.make_async_remote_copy(
        src_ref=mid_any,
        dst_ref=midw.at[:, pl.ds(own_rows, SHARE), :],
        send_sem=m_send,
        recv_sem=m_recv,
        device_id=(seq, half * 2 + 1 - core),
        device_id_type=MESH,
    )
    mid_swap.start()

    for copy, d in ((g_copies[0], 2), (g_copies[1], 1)):

        @pl.when(tile_group >= d)
        def _():
            copy.wait_recv()

        @pl.when(tile_group < d)
        def _():
            grid[2 - d] = jnp.zeros((4, 32, 128), BF16)


    @pl.when(y < 4)
    def _():
        g_copies[2].wait()


    lane = lanes_of((2, 8, 128))
    low = lane < 64
    for slot in range(3):
        for f in range(2):
            cols = []
            turned = []
            cell = grid[slot, 2 * f : 2 * f + 2].astype(F32).reshape(2, 4, 8, 128)
            for w in range(4):
                value = cell[:, w]
                cols.append(value)
                turned.append(pltpu.roll(value, 64, 2))
            for kind in range(2):
                for w in range(3):
                    if kind == 0:
                        pair = jnp.where(low, cols[w], turned[w + 1])
                    else:
                        pair = jnp.where(low, turned[w], cols[w + 1])
                    below = pltpu.roll(pair, 7, 1)
                    base = (slot * 2 + f) * 96 + kind * 48 + w * 16
                    pairs[base : base + 16, 0:128] = pair.reshape(16, 128).astype(BF16)
                    pairs[base : base + 16, 128:256] = below.reshape(16, 128).astype(BF16)

    window = jnp.concatenate([pairs[0:384], pairs[96:480], pairs[192:576]], axis=1)
    bias_in = inb_ref[...].reshape(1, 1, CH)
    gain = gain_ref[...].reshape(1, 1, CH)
    first_half = half == 0
    gain_own = jnp.where(first_half, gain[..., 0:256], gain[..., 128:384])
    shape = (4, 48, 1)
    frame = lax.broadcasted_iota(jnp.int32, shape, 0)
    line = lax.broadcasted_iota(jnp.int32, shape, 1)
    s = line & 7
    b_of = (line >> 3) & 1
    w_of = line >> 4
    for par in range(2):
        for q in range(2):
            conv = jnp.dot(window, wide[par * 2 + q], preferred_element_type=F32)
            conv = conv.reshape(4, 2, 48, CH)
            feat = conv[:, 0] + bias_in
            dfeat = conv[:, 1]
            scale_inv = lax.rsqrt(jnp.mean(feat * feat, axis=-1, keepdims=True) + 1e-06)
            along = jnp.mean(feat * dfeat, axis=-1, keepdims=True)
            feat_own = jnp.where(first_half, feat[..., 0:256], feat[..., 128:384])
            dfeat_own = jnp.where(first_half, dfeat[..., 0:256], dfeat[..., 128:384])
            normed = gain_own * feat_own * scale_inv
            tang = gain_own * scale_inv * (dfeat_own - feat_own * (scale_inv * scale_inv * along))
            sig = 1.0 / (1.0 + jnp.exp(-normed))
            act = sig * (1.0 + normed * (1.0 - sig)) * tang
            out_side = (frame < 2) & (tile_group == 0)
            if q == 0:
                out_side = out_side | ((w_of == 0) & (column == 0))
            else:
                out_side = out_side | ((w_of == 2) & (column == CG - 1))
            if par == 0:
                out_side = out_side | ((s == 0) & (2 * b_of + core == 0))
            else:
                out_side = out_side | ((s == 6) & (2 * b_of + core == 3))
            act = jnp.where(out_side, 0.0, act)
            moved = pltpu.roll(act.reshape(24, 8, 256), 7, 1).reshape(4, 3, 2, 8, 256)
            act = act.reshape(4, 3, 2, 8, 256)
            for plane, value in ((par, act), (par + 2, moved)):
                for a in range(3):
                    both = jnp.concatenate([value[a], value[a + 1]], axis=2).astype(BF16)
                    for w in range(3):
                        acts[:, plane, 2 * w + q, a] = both[w]
            keep = dfeat[2:4].reshape(2, 3, 2, 8, CH)
            keep = jnp.where(first_half, keep[:, :, 0], keep[:, :, 1])
            if par == 0:
                keep = pltpu.roll(keep.reshape(6, 8, CH), 7, 1).reshape(2, 3, 8, CH)
            for w in range(3):
                place = 2 * w + q - 1
                if 0 <= place < 4:
                    resid[1 - par, place] = keep[:, w]

    mid_copy.wait()
    mid_swap.wait()

    row = lax.broadcasted_iota(jnp.int32, (TOK, 128), 0)
    src = lax.broadcasted_iota(jnp.int32, (TOK, 128), 1)
    upper = row >= 48
    inner = jnp.where(upper, row - 48, row)
    want = ((inner >> 2) & 1) * 64 + (inner & 3) * 16 + jnp.where(upper, 8, 0) + (inner >> 3)
    order = jnp.where(src == want, 1.0, 0.0).astype(BF16)

    def mid_conv(block_of, lanes):
        acc = jnp.zeros((128, lanes.stop - lanes.start), F32)
        for a in range(3):
            for b in range(3):
                for c in range(3):
                    taken = acts[block_of, b : b + 2, c : c + 4, a].reshape(128, 256)
                    weight = midw[a * 9 + b * 3 + c, :, lanes]
                    acc = acc + jnp.dot(taken, weight, preferred_element_type=F32)
        return acc

    swaps = []
    for n, lanes in enumerate((slice(0, CH),)):
        other = mid_conv(1 - half, lanes).astype(BF16)
        sums_out[:, lanes] = jnp.dot(order, other, preferred_element_type=F32).astype(BF16)
        swaps.append(
            pltpu.make_async_remote_copy(
                src_ref=sums_out.at[:, lanes],
                dst_ref=sums_in.at[:, lanes],
                send_sem=r_send.at[n],
                recv_sem=r_recv.at[n],
                device_id=(seq, (1 - half) * 2 + core),
                device_id_type=MESH,
            )
        )
        swaps[-1].start()
    mine = mid_conv(half, slice(0, CH)) + resid[...].reshape(128, CH)
    high = mine.astype(BF16)
    low_part = (mine - high.astype(F32)).astype(BF16)
    mine = jnp.dot(order, high, preferred_element_type=F32) + jnp.dot(order, low_part, preferred_element_type=F32)
    for copy in swaps:
        copy.wait_recv()
    out_ref[...] = (mine + sums_in[...].astype(F32)).astype(BF16)

    for k in (1, 2, 3):
        to_main = lax.rem(slab + k, 2) == main_core

        @pl.when(to_main)
        def _():
            slab_copy(k, 0).wait_send()

        @pl.when(jnp.logical_not(to_main))
        def _():
            slab_copy(k, 64).wait_send()

    @pl.when(is_main)
    def _():
        for k in steps:
            y_copy(k, 32).wait_send()

    @pl.when(jnp.logical_not(is_main))
    def _():
        for k in steps:
            y_copy(k, 8).wait_send()

    for copy in sum_copies:
        copy.wait_send()
    for copy, d in ((g_copies[0], 2), (g_copies[1], 1)):

        @pl.when(group + d < GROUPS)
        def _():
            copy.wait_send()

    for copy in swaps:
        copy.wait_send()


def shards(hidden, tangent, mod_shift, mod_scale, head_weight, head_bias, in_weight, in_bias, norm_gain, mid_weight):
    any_spec = pl.BlockSpec(memory_space=pl.ANY)
    dma = pltpu.SemaphoreType.DMA
    out = pl.pallas_call(
        kernel,
        out_shape=jax.ShapeDtypeStruct((TOK, CH), BF16),
        in_specs=[any_spec] * 10,
        out_specs=pl.BlockSpec(memory_space=pltpu.VMEM),
        scratch_shapes=[
            pltpu.VMEM((TOK, DS), BF16),
            pltpu.VMEM((TOK, DS), BF16),
            pltpu.VMEM((64, DS), BF16),
            pltpu.VMEM((27, 16, CH), BF16),
            pltpu.VMEM((DS,), F32),
            pltpu.VMEM((DS,), F32),
            pltpu.VMEM((64,), F32),
            pltpu.VMEM((CH,), F32),
            pltpu.VMEM((CH,), F32),
            pltpu.VMEM((TOK, 128), BF16),
            pltpu.VMEM((3, TOK, 128), BF16),
            pltpu.VMEM((8, 128), F32),
            pltpu.VMEM((3, 8, 128), F32),
            pltpu.VMEM((CG, 32, 128), BF16),
            pltpu.VMEM((CG, 32, 128), BF16),
            pltpu.VMEM((4, 32, 128), BF16),
            pltpu.VMEM((3, 4, 32, 128), BF16),
            pltpu.VMEM((576, 256), BF16),
            pltpu.VMEM((4, 768, CH), BF16),
            pltpu.VMEM((2, 4, 6, 3, 16, 256), BF16),
            pltpu.VMEM((2, 4, 2, 8, CH), F32),
            pltpu.VMEM((27, 256, CH), BF16),
            pltpu.VMEM((TOK, CH), BF16),
            pltpu.VMEM((TOK, CH), BF16),
            pltpu.SemaphoreType.REGULAR,
            pltpu.SemaphoreType.REGULAR,
            dma((11,)),
            dma,
            dma((3,)),
            dma((3,)),
            dma((3,)),
            dma((3,)),
            dma((CG,)),
            dma((CG,)),
            dma((3,)),
            dma((3,)),
            dma,
            dma,
            dma((1,)),
            dma((1,)),
        ],
        compiler_params=pltpu.CompilerParams(collective_id=0, has_side_effects=True),
        name="decode",
    )(
        hidden,
        tangent,
        mod_shift,
        mod_scale,
        head_weight,
        head_bias,
        in_weight.reshape(27, 16, CH),
        in_bias,
        norm_gain,
        mid_weight.reshape(27, SHARE, CH),
    )
    return out.reshape(1, 2, 12, 4, CH)


def solution(mesh):
    return jax.shard_map(
        shards,
        mesh=mesh,
        in_specs=(
            P("seq", "slab"),
            P("seq", "slab"),
            P("slab"),
            P("slab"),
            P(None, "slab"),
            P(),
            P(),
            P(),
            P(),
            P(None, None, None, "slab", None),
        ),
        out_specs=P("seq", None, "slab", None, None),
        check_vma=False,
    )
```

```python
import jax
import jax.numpy as jnp
from jax import lax
from jax.experimental import pallas as pl
from jax.experimental.pallas import tpu as pltpu
from jax.sharding import PartitionSpec as P

D = 5120
CH = 384
CG = 8
GROUPS = 16
SLABS = 4
TOK = 96
DS = D // SLABS
SHARE = CH // SLABS
F32 = jnp.float32
BF16 = jnp.bfloat16
MESH = pl.DeviceIdType.MESH
NT = (((1,), (1,)), ((), ()))


def lanes_of(shape):
    return lax.broadcasted_iota(jnp.int32, shape, len(shape) - 1)


def head_partials(xv, dxv, hwv, scale_ref, shift_ref, part, sums):
    x = xv[...]
    dx = dxv[...]
    xf = x.astype(F32)
    dxf = dx.astype(F32)
    values = [
        jnp.sum(xf, axis=1, keepdims=True),
        jnp.sum(xf * xf, axis=1, keepdims=True),
        jnp.sum(dxf, axis=1, keepdims=True),
        jnp.sum(xf * dxf, axis=1, keepdims=True),
    ]
    lane = lanes_of((TOK, 128))
    moments = jnp.zeros((TOK, 128), F32)
    for k, value in enumerate(values):
        moments = jnp.where(lane == k, value, moments)
    moments = jnp.concatenate([moments, jnp.zeros((128 - TOK, 128), F32)], axis=0)
    w = hwv[...]
    wf = w.astype(F32) * (1.0 + scale_ref[...].reshape(1, DS))
    hi = wf.astype(BF16)
    lo = (wf - hi.astype(F32)).astype(BF16)
    shift = shift_ref[...].reshape(1, DS)
    shift_hi = shift.astype(BF16).astype(F32)
    shift_mid = (shift - shift_hi).astype(BF16).astype(F32)
    shift_lo = shift - shift_hi - shift_mid
    row = lax.broadcasted_iota(jnp.int32, (16, DS), 0)
    extra = jnp.where(row == 0, 1.0, 0.0)
    extra = jnp.where(row == 1, shift_hi, extra)
    extra = jnp.where(row == 2, shift_mid, extra)
    extra = jnp.where(row == 3, shift_lo, extra).astype(BF16)
    both = jnp.concatenate([x, dx, extra], axis=0)
    split = jnp.concatenate([hi, lo], axis=0)
    prod = lax.dot_general(both, split, NT, preferred_element_type=F32)
    prod = prod + pltpu.roll(prod, 64, 1)
    twice = jnp.concatenate([w, w], axis=0)
    shifted = lax.dot_general(extra, twice, NT, preferred_element_type=F32)
    weight_sum = prod[2 * TOK : 2 * TOK + 1]
    shift_sum = shifted[1:2] + shifted[2:3] + shifted[3:4]
    value = jnp.where(lane < 64, prod[0:TOK], prod[TOK : 2 * TOK])
    value = value - jnp.where(lane < 64, values[0] / DS, values[2] / DS) * weight_sum
    send = value.astype(BF16)
    part[0:64, :] = send[16:80]
    part[64:80, :] = send[0:16]
    part[80:96, :] = send[80:96]
    const = jnp.where(lanes_of((1, 128)) < 64, weight_sum, shift_sum)
    row8 = lax.broadcasted_iota(jnp.int32, (8, 128), 0)
    sums[...] = jnp.where(row8 == 4, const, jnp.transpose(moments)[0:8])
    return value


def head_finish(own, part_in, sums, bias):
    moments = jnp.concatenate([sums, jnp.zeros((96, 128), F32)], axis=0)
    moments = jnp.transpose(moments)[0:TOK]
    total = moments[:, 0:8] + moments[:, 8:16] + moments[:, 16:24] + moments[:, 24:32]
    lane = lanes_of((TOK, 128))
    lane1 = lanes_of((8, 128))
    mean = total[:, 0:1] / D
    mean_tangent = total[:, 2:3] / D
    received = part_in[0].astype(F32) + part_in[1].astype(F32) + part_in[2].astype(F32)
    part = own + jnp.concatenate([received[64:80], received[0:64], received[80:96]], axis=0)
    shift_term = jnp.zeros((1, 128), F32)
    for k in range(4):
        const = jnp.broadcast_to(sums[8 * k + 4 : 8 * k + 5], (8, 128))
        turned = pltpu.roll(const, 64, 1)
        weight_sum = jnp.where(lane1 < 64, const, turned)[0:1]
        shift_term = shift_term + turned[0:1]
        off = moments[:, 8 * k : 8 * k + 1] / DS - mean
        off_tangent = moments[:, 8 * k + 2 : 8 * k + 3] / DS - mean_tangent
        part = part + jnp.where(lane < 64, off, off_tangent) * weight_sum
    variance = total[:, 1:2] / D - mean * mean
    inverse = lax.rsqrt(variance + 1e-06)
    project = inverse * (total[:, 3:4] / D - mean * mean_tangent)
    value = inverse * part
    primal = value + shift_term + bias
    tangent = value - inverse * project * pltpu.roll(value, 64, 1)
    return jnp.where(lane < 64, primal, tangent).astype(BF16)


def kernel(
    x_any, dx_any, shift_any, scale_any, hw_any, bias_any, inw_any, inb_any, gain_any, mid_any,
    out_ref,
    xv, dxv, hwv, inwv, shift_ref, scale_ref, bias_ref, inb_ref, gain_ref, part, part_in, sums, sums_row_in, tiles, tiles_in, block, grid, pairs, wide, acts, resid,
    midw, sums_out, sums_in,
    near_sem, far_sem, load_sem, mid_sem, b_send, b_recv, x_send, x_recv, c_send, c_recv, g_send, g_recv, m_send, m_recv, r_send, r_recv,
):
    seq = lax.axis_index("seq")
    slab = lax.axis_index("slab")
    y = lax.rem(seq, CG)
    group = lax.div(seq, CG)
    core = lax.rem(slab, 2)
    half = lax.div(slab, 2)
    late = (y < 4).astype(jnp.int32)
    tile_group = lax.rem(group - late + GROUPS, GROUPS)
    column = lax.rem(y + 4, CG)

    part_in[:, 0:64, :] = jnp.zeros((3, 64, 128), BF16)
    barrier = pltpu.get_barrier_semaphore()
    z_hi = lax.div(group, 4)
    x = lax.rem(group, 4)

    def place(z_to, x_to, y_to):
        return (lax.rem(z_to, 4) * 4 + lax.rem(x_to, 4)) * CG + lax.rem(y_to, CG)

    beside_x = [(place(z_hi, x + k, y), slab) for k in (1, 3)]
    beside_z = [(place(z_hi + k, x, y), slab) for k in (1, 3)]
    beside_y = [(place(z_hi, x, y + k), slab) for k in (2, 6, 1, 7)]
    in_slab = [(seq, lax.rem(slab + k, SLABS)) for k in range(1, SLABS)]
    for device in beside_z + beside_y + beside_x + in_slab:
        pl.semaphore_signal(barrier, inc=1, device_id=device, device_id_type=MESH)

    moves = (
        (x_any.at[0:48], xv.at[0:48]),
        (x_any.at[48:96], xv.at[48:96]),
        (dx_any.at[0:48], dxv.at[0:48]),
        (dx_any.at[48:96], dxv.at[48:96]),
        (hw_any, hwv),
        (scale_any, scale_ref),
        (shift_any, shift_ref),
        (inw_any, inwv),
        (bias_any, bias_ref),
        (inb_any, inb_ref),
        (gain_any, gain_ref),
    )
    loads = [pltpu.make_async_copy(src, dst, load_sem.at[k]) for k, (src, dst) in enumerate(moves)]
    for copy in loads[0:7]:
        copy.start()

    spare = pl.multiple_of(192 - 192 * half, 64)
    midw[:, pl.ds(spare, 64), :] = jnp.zeros((27, 64, CH), BF16)
    own_rows = pl.multiple_of(half * 64 + core * SHARE, 32)
    mid_copy = pltpu.make_async_copy(mid_any, midw.at[:, pl.ds(own_rows, SHARE), :], mid_sem)

    pl.semaphore_wait(barrier, 11)
    for device in beside_z + beside_y[0:2] + beside_x:
        pl.semaphore_signal(near_sem, inc=1, device_id=device, device_id_type=MESH)

    for copy in loads[0:7]:
        copy.wait()
    for copy in loads[7:]:
        copy.start()
    mid_copy.start()
    own = head_partials(xv, dxv, hwv, scale_ref, shift_ref, part, sums)

    quarter = lax.rem(y, 4)
    main_core = lax.rem(quarter, 2)
    is_main = main_core == core

    def slab_copy(k, start):
        return pltpu.make_async_remote_copy(
            src_ref=part.at[start:TOK],
            dst_ref=part_in.at[k - 1, start:TOK],
            send_sem=b_send.at[k - 1],
            recv_sem=b_recv.at[k - 1],
            device_id=(seq, lax.rem(slab + k, SLABS)),
            device_id_type=MESH,
        )

    sum_copies = []
    for k in (2, 3, 1):
        to_main = lax.rem(slab + k, 2) == main_core
        sum_copies.append(
            pltpu.make_async_remote_copy(
                src_ref=sums,
                dst_ref=sums_row_in.at[k - 1],
                send_sem=x_send.at[k - 1],
                recv_sem=x_recv.at[k - 1],
                device_id=(seq, lax.rem(slab + k, SLABS)),
                device_id_type=MESH,
            )
        )
        sum_copies[-1].start()

        @pl.when(to_main)
        def _():
            slab_copy(k, 0).start()

        @pl.when(jnp.logical_not(to_main))
        def _():
            slab_copy(k, 64).start()

    row = lax.broadcasted_iota(jnp.int32, (256, TOK), 0)
    token = lax.broadcasted_iota(jnp.int32, (256, TOK), 1)
    line = row & 31
    t = line & 7
    main_row = jnp.where((t == 0) | (t == 7), -1, t - 1)
    edge_row = jnp.where(line < 8, jnp.where((line & 1) == 0, 5, 0), -1)
    src_row = jnp.where(is_main, main_row, edge_row)
    col = 2 * (((row >> 5) + 4) & 7) - 1 + jnp.where(is_main, line >> 3, line >> 1)
    hit = (src_row >= 0) & (col >= 0) & (col < 16) & (token == src_row * 16 + col)
    pick = jnp.where(hit, 1.0, 0.0).astype(BF16)

    @pl.when(is_main)
    def _():
        for k in (1, 3, 2):
            slab_copy(k, 0).wait_recv()

    @pl.when(jnp.logical_not(is_main))
    def _():
        for k in (1, 3, 2):
            slab_copy(k, 64).wait_recv()

    for copy in sum_copies:
        copy.wait_recv()
    all_sums = jnp.concatenate([sums[...], sums_row_in[0], sums_row_in[1], sums_row_in[2]], axis=0)
    loads[8].wait()
    bias = bias_ref[...].reshape(1, 64)
    patches = head_finish(own, part_in, all_sums, jnp.concatenate([bias, bias], axis=1))
    spread = jnp.dot(pick, patches, preferred_element_type=F32).astype(BF16)
    tiles[...] = spread.reshape(CG, 32, 128)

    pl.semaphore_wait(near_sem, 6)
    for device in beside_x:
        pl.semaphore_signal(far_sem, inc=1, device_id=device, device_id_type=MESH)

    def y_copy(k, rows):
        to = lax.rem(y + k, CG)
        return pltpu.make_async_remote_copy(
            src_ref=tiles.at[to, 0:rows],
            dst_ref=tiles_in.at[y, 0:rows],
            send_sem=c_send.at[k],
            recv_sem=c_recv.at[k],
            device_id=(group * CG + to, slab),
            device_id_type=MESH,
        )

    steps = (4, 3, 5, 2, 6, 1, 7)

    @pl.when(is_main)
    def _():
        for k in steps:
            y_copy(k, 32).start()

    @pl.when(jnp.logical_not(is_main))
    def _():
        for k in steps:
            y_copy(k, 8).start()

    tiles_in[y] = tiles[y]

    @pl.when(is_main)
    def _():
        for k in steps:
            y_copy(k, 8 if k % 2 else 32).wait_recv()

    @pl.when(jnp.logical_not(is_main))
    def _():
        for k in steps:
            y_copy(k, 32 if k % 2 else 8).wait_recv()

    to_row = lax.broadcasted_iota(jnp.int32, (32, 48), 0)
    from_row = lax.broadcasted_iota(jnp.int32, (32, 48), 1)
    col2 = (to_row >> 3) * 2
    t = to_row & 7
    for b in range(2):
        q = 2 * b + core
        joined = (to_row == from_row) | ((t == 0) & (from_row == 32 + col2) & (q > 0))
        joined = joined | ((t == 7) & (from_row == 41 + col2) & (q < 3))
        join = jnp.where(joined, 1.0, 0.0).astype(BF16)
        for f in range(2):
            main = tiles_in[4 * f + q].astype(F32)
            above = tiles_in[4 * f + jnp.maximum(q - 1, 0), 0:8].astype(F32)
            below = tiles_in[4 * f + jnp.minimum(q + 1, 3), 0:8].astype(F32)
            value = jnp.concatenate([main, above, below], axis=0).astype(BF16)
            block[f * 2 + b] = jnp.dot(join, value, preferred_element_type=F32).astype(BF16)

    g_copies = []
    for d in (2, 1, 0):
        g_copies.append(
            pltpu.make_async_remote_copy(
                src_ref=block,
                dst_ref=grid.at[2 - d],
                send_sem=g_send.at[d],
                recv_sem=g_recv.at[d],
                device_id=(lax.rem(group + d + late, GROUPS) * CG + y, slab),
                device_id_type=MESH,
            )
        )
    pl.semaphore_wait(far_sem, 2)
    for copy, d in ((g_copies[0], 2), (g_copies[1], 1)):

        @pl.when(group + d < GROUPS)
        def _():
            copy.start()


    @pl.when(y < 4)
    def _():
        g_copies[2].start()

    @pl.when(y >= 4)
    def _():
        grid[2] = block[...]

    mid_swap = pltpu.make_async_remote_copy(
        src_ref=mid_any,
        dst_ref=midw.at[:, pl.ds(own_rows, SHARE), :],
        send_sem=m_send,
        recv_sem=m_recv,
        device_id=(seq, half * 2 + 1 - core),
        device_id_type=MESH,
    )
    mid_swap.start()

    for copy in (loads[7], loads[9], loads[10]):
        copy.wait()
    for par in range(2):
        for q in range(2):
            for a in range(3):
                for i in range(4):
                    for j in range(4):
                        tap_row, tap_col = (i - par, j - q)
                        cell = (i // 2) * 8 + (j // 2) * 4 + (i % 2) * 2 + j % 2
                        rows = slice(a * 256 + cell * 16, a * 256 + cell * 16 + 16)
                        if 0 <= tap_row < 3 and 0 <= tap_col < 3:
                            piece = inwv[a * 9 + tap_row * 3 + tap_col]
                        else:
                            piece = jnp.zeros((16, CH), BF16)
                        wide[par * 2 + q, rows, :] = piece

    for copy, d in ((g_copies[0], 2), (g_copies[1], 1)):

        @pl.when(tile_group >= d)
        def _():
            copy.wait_recv()

        @pl.when(tile_group < d)
        def _():
            grid[2 - d] = jnp.zeros((4, 32, 128), BF16)


    @pl.when(y < 4)
    def _():
        g_copies[2].wait()


    lane = lanes_of((2, 8, 128))
    low = lane < 64
    for slot in range(3):
        for f in range(2):
            cols = []
            turned = []
            cell = grid[slot, 2 * f : 2 * f + 2].astype(F32).reshape(2, 4, 8, 128)
            for w in range(4):
                value = cell[:, w]
                cols.append(value)
                turned.append(pltpu.roll(value, 64, 2))
            for kind in range(2):
                for w in range(3):
                    if kind == 0:
                        pair = jnp.where(low, cols[w], turned[w + 1])
                    else:
                        pair = jnp.where(low, turned[w], cols[w + 1])
                    below = pltpu.roll(pair, 7, 1)
                    base = (slot * 2 + f) * 96 + kind * 48 + w * 16
                    pairs[base : base + 16, 0:128] = pair.reshape(16, 128).astype(BF16)
                    pairs[base : base + 16, 128:256] = below.reshape(16, 128).astype(BF16)

    window = jnp.concatenate([pairs[0:384], pairs[96:480], pairs[192:576]], axis=1)
    bias_in = inb_ref[...].reshape(1, 1, CH)
    gain = gain_ref[...].reshape(1, 1, CH)
    first_half = half == 0
    gain_own = jnp.where(first_half, gain[..., 0:256], gain[..., 128:384])
    shape = (4, 48, 1)
    frame = lax.broadcasted_iota(jnp.int32, shape, 0)
    line = lax.broadcasted_iota(jnp.int32, shape, 1)
    s = line & 7
    b_of = (line >> 3) & 1
    w_of = line >> 4
    for par in range(2):
        for q in range(2):
            conv = jnp.dot(window, wide[par * 2 + q], preferred_element_type=F32)
            conv = conv.reshape(4, 2, 48, CH)
            feat = conv[:, 0] + bias_in
            dfeat = conv[:, 1]
            scale_inv = lax.rsqrt(jnp.mean(feat * feat, axis=-1, keepdims=True) + 1e-06)
            along = jnp.mean(feat * dfeat, axis=-1, keepdims=True)
            feat_own = jnp.where(first_half, feat[..., 0:256], feat[..., 128:384])
            dfeat_own = jnp.where(first_half, dfeat[..., 0:256], dfeat[..., 128:384])
            normed = gain_own * feat_own * scale_inv
            tang = gain_own * scale_inv * (dfeat_own - feat_own * (scale_inv * scale_inv * along))
            sig = 1.0 / (1.0 + jnp.exp(-normed))
            act = sig * (1.0 + normed * (1.0 - sig)) * tang
            out_side = (frame < 2) & (tile_group == 0)
            if q == 0:
                out_side = out_side | ((w_of == 0) & (column == 0))
            else:
                out_side = out_side | ((w_of == 2) & (column == CG - 1))
            if par == 0:
                out_side = out_side | ((s == 0) & (2 * b_of + core == 0))
            else:
                out_side = out_side | ((s == 6) & (2 * b_of + core == 3))
            act = jnp.where(out_side, 0.0, act)
            moved = pltpu.roll(act.reshape(24, 8, 256), 7, 1).reshape(4, 3, 2, 8, 256)
            act = act.reshape(4, 3, 2, 8, 256)
            for plane, value in ((par, act), (par + 2, moved)):
                for a in range(3):
                    both = jnp.concatenate([value[a], value[a + 1]], axis=2).astype(BF16)
                    for w in range(3):
                        acts[:, plane, 2 * w + q, a] = both[w]
            keep = dfeat[2:4].reshape(2, 3, 2, 8, CH)
            keep = jnp.where(first_half, keep[:, :, 0], keep[:, :, 1])
            if par == 0:
                keep = pltpu.roll(keep.reshape(6, 8, CH), 7, 1).reshape(2, 3, 8, CH)
            for w in range(3):
                place = 2 * w + q - 1
                if 0 <= place < 4:
                    resid[1 - par, place] = keep[:, w]

    mid_copy.wait()
    mid_swap.wait()

    row = lax.broadcasted_iota(jnp.int32, (TOK, 128), 0)
    src = lax.broadcasted_iota(jnp.int32, (TOK, 128), 1)
    upper = row >= 48
    inner = jnp.where(upper, row - 48, row)
    want = ((inner >> 2) & 1) * 64 + (inner & 3) * 16 + jnp.where(upper, 8, 0) + (inner >> 3)
    order = jnp.where(src == want, 1.0, 0.0).astype(BF16)

    def mid_conv(block_of, lanes):
        acc = jnp.zeros((128, lanes.stop - lanes.start), F32)
        for a in range(3):
            for b in range(3):
                for c in range(3):
                    taken = acts[block_of, b : b + 2, c : c + 4, a].reshape(128, 256)
                    weight = midw[a * 9 + b * 3 + c, :, lanes]
                    acc = acc + jnp.dot(taken, weight, preferred_element_type=F32)
        return acc

    swaps = []
    for n, lanes in enumerate((slice(0, CH),)):
        other = mid_conv(1 - half, lanes).astype(BF16)
        sums_out[:, lanes] = jnp.dot(order, other, preferred_element_type=F32).astype(BF16)
        swaps.append(
            pltpu.make_async_remote_copy(
                src_ref=sums_out.at[:, lanes],
                dst_ref=sums_in.at[:, lanes],
                send_sem=r_send.at[n],
                recv_sem=r_recv.at[n],
                device_id=(seq, (1 - half) * 2 + core),
                device_id_type=MESH,
            )
        )
        swaps[-1].start()
    mine = mid_conv(half, slice(0, CH)) + resid[...].reshape(128, CH)
    high = mine.astype(BF16)
    low_part = (mine - high.astype(F32)).astype(BF16)
    mine = jnp.dot(order, high, preferred_element_type=F32) + jnp.dot(order, low_part, preferred_element_type=F32)
    for copy in swaps:
        copy.wait_recv()
    out_ref[...] = (mine + sums_in[...].astype(F32)).astype(BF16)

    for k in (1, 2, 3):
        to_main = lax.rem(slab + k, 2) == main_core

        @pl.when(to_main)
        def _():
            slab_copy(k, 0).wait_send()

        @pl.when(jnp.logical_not(to_main))
        def _():
            slab_copy(k, 64).wait_send()

    @pl.when(is_main)
    def _():
        for k in steps:
            y_copy(k, 32).wait_send()

    @pl.when(jnp.logical_not(is_main))
    def _():
        for k in steps:
            y_copy(k, 8).wait_send()

    for copy in sum_copies:
        copy.wait_send()
    for copy, d in ((g_copies[0], 2), (g_copies[1], 1)):

        @pl.when(group + d < GROUPS)
        def _():
            copy.wait_send()

    for copy in swaps:
        copy.wait_send()


def shards(hidden, tangent, mod_shift, mod_scale, head_weight, head_bias, in_weight, in_bias, norm_gain, mid_weight):
    any_spec = pl.BlockSpec(memory_space=pl.ANY)
    dma = pltpu.SemaphoreType.DMA
    out = pl.pallas_call(
        kernel,
        out_shape=jax.ShapeDtypeStruct((TOK, CH), BF16),
        in_specs=[any_spec] * 10,
        out_specs=pl.BlockSpec(memory_space=pltpu.VMEM),
        scratch_shapes=[
            pltpu.VMEM((TOK, DS), BF16),
            pltpu.VMEM((TOK, DS), BF16),
            pltpu.VMEM((64, DS), BF16),
            pltpu.VMEM((27, 16, CH), BF16),
            pltpu.VMEM((DS,), F32),
            pltpu.VMEM((DS,), F32),
            pltpu.VMEM((64,), F32),
            pltpu.VMEM((CH,), F32),
            pltpu.VMEM((CH,), F32),
            pltpu.VMEM((TOK, 128), BF16),
            pltpu.VMEM((3, TOK, 128), BF16),
            pltpu.VMEM((8, 128), F32),
            pltpu.VMEM((3, 8, 128), F32),
            pltpu.VMEM((CG, 32, 128), BF16),
            pltpu.VMEM((CG, 32, 128), BF16),
            pltpu.VMEM((4, 32, 128), BF16),
            pltpu.VMEM((3, 4, 32, 128), BF16),
            pltpu.VMEM((576, 256), BF16),
            pltpu.VMEM((4, 768, CH), BF16),
            pltpu.VMEM((2, 4, 6, 3, 16, 256), BF16),
            pltpu.VMEM((2, 4, 2, 8, CH), F32),
            pltpu.VMEM((27, 256, CH), BF16),
            pltpu.VMEM((TOK, CH), BF16),
            pltpu.VMEM((TOK, CH), BF16),
            pltpu.SemaphoreType.REGULAR,
            pltpu.SemaphoreType.REGULAR,
            dma((11,)),
            dma,
            dma((3,)),
            dma((3,)),
            dma((3,)),
            dma((3,)),
            dma((CG,)),
            dma((CG,)),
            dma((3,)),
            dma((3,)),
            dma,
            dma,
            dma((1,)),
            dma((1,)),
        ],
        compiler_params=pltpu.CompilerParams(collective_id=0, has_side_effects=True),
        name="decode",
    )(
        hidden,
        tangent,
        mod_shift,
        mod_scale,
        head_weight,
        head_bias,
        in_weight.reshape(27, 16, CH),
        in_bias,
        norm_gain,
        mid_weight.reshape(27, SHARE, CH),
    )
    return out.reshape(1, 2, 12, 4, CH)


def solution(mesh):
    return jax.shard_map(
        shards,
        mesh=mesh,
        in_specs=(
            P("seq", "slab"),
            P("seq", "slab"),
            P("slab"),
            P("slab"),
            P(None, "slab"),
            P(),
            P(),
            P(),
            P(),
            P(None, None, None, "slab", None),
        ),
        out_specs=P("seq", None, "slab", None, None),
        check_vma=False,
    )
```

```python
import jax
import jax.numpy as jnp
from jax import lax
from jax.experimental import pallas as pl
from jax.experimental.pallas import tpu as pltpu
from jax.sharding import PartitionSpec as P

D = 5120
CH = 384
CG = 8
GROUPS = 16
SLABS = 4
TOK = 96
DS = D // SLABS
SHARE = CH // SLABS
F32 = jnp.float32
BF16 = jnp.bfloat16
MESH = pl.DeviceIdType.MESH
NT = (((1,), (1,)), ((), ()))


def lanes_of(shape):
    return lax.broadcasted_iota(jnp.int32, shape, len(shape) - 1)


def head_partials(xv, dxv, hwv, scale_ref, shift_ref, part, sums):
    x = xv[...]
    dx = dxv[...]
    xf = x.astype(F32)
    dxf = dx.astype(F32)
    values = [
        jnp.sum(xf, axis=1, keepdims=True),
        jnp.sum(xf * xf, axis=1, keepdims=True),
        jnp.sum(dxf, axis=1, keepdims=True),
        jnp.sum(xf * dxf, axis=1, keepdims=True),
    ]
    lane = lanes_of((TOK, 128))
    moments = jnp.zeros((TOK, 128), F32)
    for k, value in enumerate(values):
        moments = jnp.where(lane == k, value, moments)
    moments = jnp.concatenate([moments, jnp.zeros((128 - TOK, 128), F32)], axis=0)
    w = hwv[...]
    wf = w.astype(F32) * (1.0 + scale_ref[...].reshape(1, DS))
    hi = wf.astype(BF16)
    lo = (wf - hi.astype(F32)).astype(BF16)
    shift = shift_ref[...].reshape(1, DS)
    shift_hi = shift.astype(BF16).astype(F32)
    shift_mid = (shift - shift_hi).astype(BF16).astype(F32)
    shift_lo = shift - shift_hi - shift_mid
    row = lax.broadcasted_iota(jnp.int32, (16, DS), 0)
    extra = jnp.where(row == 0, 1.0, 0.0)
    extra = jnp.where(row == 1, shift_hi, extra)
    extra = jnp.where(row == 2, shift_mid, extra)
    extra = jnp.where(row == 3, shift_lo, extra).astype(BF16)
    both = jnp.concatenate([x, dx, extra], axis=0)
    split = jnp.concatenate([hi, lo], axis=0)
    prod = lax.dot_general(both, split, NT, preferred_element_type=F32)
    prod = prod + pltpu.roll(prod, 64, 1)
    twice = jnp.concatenate([w, w], axis=0)
    shifted = lax.dot_general(extra, twice, NT, preferred_element_type=F32)
    weight_sum = prod[2 * TOK : 2 * TOK + 1]
    shift_sum = shifted[1:2] + shifted[2:3] + shifted[3:4]
    value = jnp.where(lane < 64, prod[0:TOK], prod[TOK : 2 * TOK])
    value = value - jnp.where(lane < 64, values[0] / DS, values[2] / DS) * weight_sum
    send = value.astype(BF16)
    part[0:64, :] = send[16:80]
    part[64:80, :] = send[0:16]
    part[80:96, :] = send[80:96]
    const = jnp.where(lanes_of((1, 128)) < 64, weight_sum, shift_sum)
    row8 = lax.broadcasted_iota(jnp.int32, (8, 128), 0)
    sums[...] = jnp.where(row8 == 4, const, jnp.transpose(moments)[0:8])
    return value


def head_finish(own, part_in, sums, bias):
    moments = jnp.concatenate([sums, jnp.zeros((96, 128), F32)], axis=0)
    moments = jnp.transpose(moments)[0:TOK]
    total = moments[:, 0:8] + moments[:, 8:16] + moments[:, 16:24] + moments[:, 24:32]
    lane = lanes_of((TOK, 128))
    lane1 = lanes_of((8, 128))
    mean = total[:, 0:1] / D
    mean_tangent = total[:, 2:3] / D
    received = part_in[0].astype(F32) + part_in[1].astype(F32) + part_in[2].astype(F32)
    part = own + jnp.concatenate([received[64:80], received[0:64], received[80:96]], axis=0)
    shift_term = jnp.zeros((1, 128), F32)
    for k in range(4):
        const = jnp.broadcast_to(sums[8 * k + 4 : 8 * k + 5], (8, 128))
        turned = pltpu.roll(const, 64, 1)
        weight_sum = jnp.where(lane1 < 64, const, turned)[0:1]
        shift_term = shift_term + turned[0:1]
        off = moments[:, 8 * k : 8 * k + 1] / DS - mean
        off_tangent = moments[:, 8 * k + 2 : 8 * k + 3] / DS - mean_tangent
        part = part + jnp.where(lane < 64, off, off_tangent) * weight_sum
    variance = total[:, 1:2] / D - mean * mean
    inverse = lax.rsqrt(variance + 1e-06)
    project = inverse * (total[:, 3:4] / D - mean * mean_tangent)
    value = inverse * part
    primal = value + shift_term + bias
    tangent = value - inverse * project * pltpu.roll(value, 64, 1)
    return jnp.where(lane < 64, primal, tangent).astype(BF16)


def kernel(
    x_any, dx_any, shift_any, scale_any, hw_any, bias_any, inw_any, inb_any, gain_any, mid_any,
    out_ref,
    xv, dxv, hwv, inwv, shift_ref, scale_ref, bias_ref, inb_ref, gain_ref, part, part_in, sums, sums_row_in, tiles, tiles_in, block, grid, pairs, wide, acts, resid,
    midw, sums_out, sums_in,
    near_sem, far_sem, load_sem, mid_sem, b_send, b_recv, x_send, x_recv, c_send, c_recv, g_send, g_recv, m_send, m_recv, r_send, r_recv,
):
    seq = lax.axis_index("seq")
    slab = lax.axis_index("slab")
    y = lax.rem(seq, CG)
    group = lax.div(seq, CG)
    core = lax.rem(slab, 2)
    half = lax.div(slab, 2)
    late = (y < 4).astype(jnp.int32)
    tile_group = lax.rem(group - late + GROUPS, GROUPS)
    column = lax.rem(y + 4, CG)

    part_in[:, 0:64, :] = jnp.zeros((3, 64, 128), BF16)
    barrier = pltpu.get_barrier_semaphore()
    z_hi = lax.div(group, 4)
    x = lax.rem(group, 4)

    def place(z_to, x_to, y_to):
        return (lax.rem(z_to, 4) * 4 + lax.rem(x_to, 4)) * CG + lax.rem(y_to, CG)

    beside_x = [(place(z_hi, x + k, y), slab) for k in (1, 3)]
    beside_z = [(place(z_hi + k, x, y), slab) for k in (1, 3)]
    beside_y = [(place(z_hi, x, y + k), slab) for k in (2, 6, 1, 7)]
    in_slab = [(seq, lax.rem(slab + k, SLABS)) for k in range(1, SLABS)]
    for device in beside_z + beside_y + beside_x + in_slab:
        pl.semaphore_signal(barrier, inc=1, device_id=device, device_id_type=MESH)

    moves = (
        (x_any.at[0:48], xv.at[0:48]),
        (x_any.at[48:96], xv.at[48:96]),
        (dx_any.at[0:48], dxv.at[0:48]),
        (dx_any.at[48:96], dxv.at[48:96]),
        (hw_any, hwv),
        (scale_any, scale_ref),
        (shift_any, shift_ref),
        (inw_any, inwv),
        (bias_any, bias_ref),
        (inb_any, inb_ref),
        (gain_any, gain_ref),
    )
    loads = [pltpu.make_async_copy(src, dst, load_sem.at[k]) for k, (src, dst) in enumerate(moves)]
    for copy in loads[0:7]:
        copy.start()

    spare = pl.multiple_of(192 - 192 * half, 64)
    midw[:, pl.ds(spare, 64), :] = jnp.zeros((27, 64, CH), BF16)
    own_rows = pl.multiple_of(half * 64 + core * SHARE, 32)
    mid_copy = pltpu.make_async_copy(mid_any, midw.at[:, pl.ds(own_rows, SHARE), :], mid_sem)

    pl.semaphore_wait(barrier, 11)
    for device in beside_z + beside_y[0:2] + beside_x:
        pl.semaphore_signal(near_sem, inc=1, device_id=device, device_id_type=MESH)

    for copy in loads[0:7]:
        copy.wait()
    own = head_partials(xv, dxv, hwv, scale_ref, shift_ref, part, sums)

    quarter = lax.rem(y, 4)
    main_core = lax.rem(quarter, 2)
    is_main = main_core == core

    def slab_copy(k, start):
        return pltpu.make_async_remote_copy(
            src_ref=part.at[start:TOK],
            dst_ref=part_in.at[k - 1, start:TOK],
            send_sem=b_send.at[k - 1],
            recv_sem=b_recv.at[k - 1],
            device_id=(seq, lax.rem(slab + k, SLABS)),
            device_id_type=MESH,
        )

    sum_copies = []
    for k in (2, 3, 1):
        to_main = lax.rem(slab + k, 2) == main_core
        sum_copies.append(
            pltpu.make_async_remote_copy(
                src_ref=sums,
                dst_ref=sums_row_in.at[k - 1],
                send_sem=x_send.at[k - 1],
                recv_sem=x_recv.at[k - 1],
                device_id=(seq, lax.rem(slab + k, SLABS)),
                device_id_type=MESH,
            )
        )
        sum_copies[-1].start()

        @pl.when(to_main)
        def _():
            slab_copy(k, 0).start()

        @pl.when(jnp.logical_not(to_main))
        def _():
            slab_copy(k, 64).start()

    for copy in loads[7:]:
        copy.start()

    row = lax.broadcasted_iota(jnp.int32, (256, TOK), 0)
    token = lax.broadcasted_iota(jnp.int32, (256, TOK), 1)
    line = row & 31
    t = line & 7
    main_row = jnp.where((t == 0) | (t == 7), -1, t - 1)
    edge_row = jnp.where(line < 8, jnp.where((line & 1) == 0, 5, 0), -1)
    src_row = jnp.where(is_main, main_row, edge_row)
    col = 2 * (((row >> 5) + 4) & 7) - 1 + jnp.where(is_main, line >> 3, line >> 1)
    hit = (src_row >= 0) & (col >= 0) & (col < 16) & (token == src_row * 16 + col)
    pick = jnp.where(hit, 1.0, 0.0).astype(BF16)

    @pl.when(is_main)
    def _():
        for k in (1, 3, 2):
            slab_copy(k, 0).wait_recv()

    @pl.when(jnp.logical_not(is_main))
    def _():
        for k in (1, 3, 2):
            slab_copy(k, 64).wait_recv()

    for copy in sum_copies:
        copy.wait_recv()
    all_sums = jnp.concatenate([sums[...], sums_row_in[0], sums_row_in[1], sums_row_in[2]], axis=0)
    loads[8].wait()
    bias = bias_ref[...].reshape(1, 64)
    patches = head_finish(own, part_in, all_sums, jnp.concatenate([bias, bias], axis=1))
    spread = jnp.dot(pick, patches, preferred_element_type=F32).astype(BF16)
    tiles[...] = spread.reshape(CG, 32, 128)

    pl.semaphore_wait(near_sem, 6)
    for device in beside_x:
        pl.semaphore_signal(far_sem, inc=1, device_id=device, device_id_type=MESH)

    def y_copy(k, rows):
        to = lax.rem(y + k, CG)
        return pltpu.make_async_remote_copy(
            src_ref=tiles.at[to, 0:rows],
            dst_ref=tiles_in.at[y, 0:rows],
            send_sem=c_send.at[k],
            recv_sem=c_recv.at[k],
            device_id=(group * CG + to, slab),
            device_id_type=MESH,
        )

    steps = (4, 3, 5, 2, 6, 1, 7)

    @pl.when(is_main)
    def _():
        for k in steps:
            y_copy(k, 32).start()

    @pl.when(jnp.logical_not(is_main))
    def _():
        for k in steps:
            y_copy(k, 8).start()

    tiles_in[y] = tiles[y]

    @pl.when(is_main)
    def _():
        for k in steps:
            y_copy(k, 8 if k % 2 else 32).wait_recv()

    @pl.when(jnp.logical_not(is_main))
    def _():
        for k in steps:
            y_copy(k, 32 if k % 2 else 8).wait_recv()

    to_row = lax.broadcasted_iota(jnp.int32, (32, 48), 0)
    from_row = lax.broadcasted_iota(jnp.int32, (32, 48), 1)
    col2 = (to_row >> 3) * 2
    t = to_row & 7
    for b in range(2):
        q = 2 * b + core
        joined = (to_row == from_row) | ((t == 0) & (from_row == 32 + col2) & (q > 0))
        joined = joined | ((t == 7) & (from_row == 41 + col2) & (q < 3))
        join = jnp.where(joined, 1.0, 0.0).astype(BF16)
        for f in range(2):
            main = tiles_in[4 * f + q].astype(F32)
            above = tiles_in[4 * f + jnp.maximum(q - 1, 0), 0:8].astype(F32)
            below = tiles_in[4 * f + jnp.minimum(q + 1, 3), 0:8].astype(F32)
            value = jnp.concatenate([main, above, below], axis=0).astype(BF16)
            block[f * 2 + b] = jnp.dot(join, value, preferred_element_type=F32).astype(BF16)

    g_copies = []
    for d in (2, 1, 0):
        g_copies.append(
            pltpu.make_async_remote_copy(
                src_ref=block,
                dst_ref=grid.at[2 - d],
                send_sem=g_send.at[d],
                recv_sem=g_recv.at[d],
                device_id=(lax.rem(group + d + late, GROUPS) * CG + y, slab),
                device_id_type=MESH,
            )
        )
    pl.semaphore_wait(far_sem, 2)
    for copy, d in ((g_copies[0], 2), (g_copies[1], 1)):

        @pl.when(group + d < GROUPS)
        def _():
            copy.start()


    @pl.when(y < 4)
    def _():
        g_copies[2].start()

    @pl.when(y >= 4)
    def _():
        grid[2] = block[...]

    mid_swap = pltpu.make_async_remote_copy(
        src_ref=mid_any,
        dst_ref=midw.at[:, pl.ds(own_rows, SHARE), :],
        send_sem=m_send,
        recv_sem=m_recv,
        device_id=(seq, half * 2 + 1 - core),
        device_id_type=MESH,
    )
    mid_copy.start()
    mid_swap.start()

    for copy in (loads[7], loads[9], loads[10]):
        copy.wait()
    for par in range(2):
        for q in range(2):
            for a in range(3):
                for i in range(4):
                    for j in range(4):
                        tap_row, tap_col = (i - par, j - q)
                        cell = (i // 2) * 8 + (j // 2) * 4 + (i % 2) * 2 + j % 2
                        rows = slice(a * 256 + cell * 16, a * 256 + cell * 16 + 16)
                        if 0 <= tap_row < 3 and 0 <= tap_col < 3:
                            piece = inwv[a * 9 + tap_row * 3 + tap_col]
                        else:
                            piece = jnp.zeros((16, CH), BF16)
                        wide[par * 2 + q, rows, :] = piece

    for copy, d in ((g_copies[0], 2), (g_copies[1], 1)):

        @pl.when(tile_group >= d)
        def _():
            copy.wait_recv()

        @pl.when(tile_group < d)
        def _():
            grid[2 - d] = jnp.zeros((4, 32, 128), BF16)


    @pl.when(y < 4)
    def _():
        g_copies[2].wait()


    lane = lanes_of((2, 8, 128))
    low = lane < 64
    for slot in range(3):
        for f in range(2):
            cols = []
            turned = []
            cell = grid[slot, 2 * f : 2 * f + 2].astype(F32).reshape(2, 4, 8, 128)
            for w in range(4):
                value = cell[:, w]
                cols.append(value)
                turned.append(pltpu.roll(value, 64, 2))
            for kind in range(2):
                for w in range(3):
                    if kind == 0:
                        pair = jnp.where(low, cols[w], turned[w + 1])
                    else:
                        pair = jnp.where(low, turned[w], cols[w + 1])
                    below = pltpu.roll(pair, 7, 1)
                    base = (slot * 2 + f) * 96 + kind * 48 + w * 16
                    pairs[base : base + 16, 0:128] = pair.reshape(16, 128).astype(BF16)
                    pairs[base : base + 16, 128:256] = below.reshape(16, 128).astype(BF16)

    window = jnp.concatenate([pairs[0:384], pairs[96:480], pairs[192:576]], axis=1)
    bias_in = inb_ref[...].reshape(1, 1, CH)
    gain = gain_ref[...].reshape(1, 1, CH)
    first_half = half == 0
    gain_own = jnp.where(first_half, gain[..., 0:256], gain[..., 128:384])
    shape = (4, 48, 1)
    frame = lax.broadcasted_iota(jnp.int32, shape, 0)
    line = lax.broadcasted_iota(jnp.int32, shape, 1)
    s = line & 7
    b_of = (line >> 3) & 1
    w_of = line >> 4
    for par in range(2):
        for q in range(2):
            conv = jnp.dot(window, wide[par * 2 + q], preferred_element_type=F32)
            conv = conv.reshape(4, 2, 48, CH)
            feat = conv[:, 0] + bias_in
            dfeat = conv[:, 1]
            scale_inv = lax.rsqrt(jnp.mean(feat * feat, axis=-1, keepdims=True) + 1e-06)
            along = jnp.mean(feat * dfeat, axis=-1, keepdims=True)
            feat_own = jnp.where(first_half, feat[..., 0:256], feat[..., 128:384])
            dfeat_own = jnp.where(first_half, dfeat[..., 0:256], dfeat[..., 128:384])
            normed = gain_own * feat_own * scale_inv
            tang = gain_own * scale_inv * (dfeat_own - feat_own * (scale_inv * scale_inv * along))
            sig = 1.0 / (1.0 + jnp.exp(-normed))
            act = sig * (1.0 + normed * (1.0 - sig)) * tang
            out_side = (frame < 2) & (tile_group == 0)
            if q == 0:
                out_side = out_side | ((w_of == 0) & (column == 0))
            else:
                out_side = out_side | ((w_of == 2) & (column == CG - 1))
            if par == 0:
                out_side = out_side | ((s == 0) & (2 * b_of + core == 0))
            else:
                out_side = out_side | ((s == 6) & (2 * b_of + core == 3))
            act = jnp.where(out_side, 0.0, act)
            moved = pltpu.roll(act.reshape(24, 8, 256), 7, 1).reshape(4, 3, 2, 8, 256)
            act = act.reshape(4, 3, 2, 8, 256)
            for plane, value in ((par, act), (par + 2, moved)):
                for a in range(3):
                    both = jnp.concatenate([value[a], value[a + 1]], axis=2).astype(BF16)
                    for w in range(3):
                        acts[:, plane, 2 * w + q, a] = both[w]
            keep = dfeat[2:4].reshape(2, 3, 2, 8, CH)
            keep = jnp.where(first_half, keep[:, :, 0], keep[:, :, 1])
            if par == 0:
                keep = pltpu.roll(keep.reshape(6, 8, CH), 7, 1).reshape(2, 3, 8, CH)
            for w in range(3):
                place = 2 * w + q - 1
                if 0 <= place < 4:
                    resid[1 - par, place] = keep[:, w]

    mid_copy.wait()
    mid_swap.wait()

    row = lax.broadcasted_iota(jnp.int32, (TOK, 128), 0)
    src = lax.broadcasted_iota(jnp.int32, (TOK, 128), 1)
    upper = row >= 48
    inner = jnp.where(upper, row - 48, row)
    want = ((inner >> 2) & 1) * 64 + (inner & 3) * 16 + jnp.where(upper, 8, 0) + (inner >> 3)
    order = jnp.where(src == want, 1.0, 0.0).astype(BF16)

    def mid_conv(block_of, lanes):
        acc = jnp.zeros((128, lanes.stop - lanes.start), F32)
        for a in range(3):
            for b in range(3):
                for c in range(3):
                    taken = acts[block_of, b : b + 2, c : c + 4, a].reshape(128, 256)
                    weight = midw[a * 9 + b * 3 + c, :, lanes]
                    acc = acc + jnp.dot(taken, weight, preferred_element_type=F32)
        return acc

    swaps = []
    for n, lanes in enumerate((slice(0, CH),)):
        other = mid_conv(1 - half, lanes).astype(BF16)
        sums_out[:, lanes] = jnp.dot(order, other, preferred_element_type=F32).astype(BF16)
        swaps.append(
            pltpu.make_async_remote_copy(
                src_ref=sums_out.at[:, lanes],
                dst_ref=sums_in.at[:, lanes],
                send_sem=r_send.at[n],
                recv_sem=r_recv.at[n],
                device_id=(seq, (1 - half) * 2 + core),
                device_id_type=MESH,
            )
        )
        swaps[-1].start()
    mine = mid_conv(half, slice(0, CH)) + resid[...].reshape(128, CH)
    high = mine.astype(BF16)
    low_part = (mine - high.astype(F32)).astype(BF16)
    mine = jnp.dot(order, high, preferred_element_type=F32) + jnp.dot(order, low_part, preferred_element_type=F32)
    for copy in swaps:
        copy.wait_recv()
    out_ref[...] = (mine + sums_in[...].astype(F32)).astype(BF16)

    for k in (1, 2, 3):
        to_main = lax.rem(slab + k, 2) == main_core

        @pl.when(to_main)
        def _():
            slab_copy(k, 0).wait_send()

        @pl.when(jnp.logical_not(to_main))
        def _():
            slab_copy(k, 64).wait_send()

    @pl.when(is_main)
    def _():
        for k in steps:
            y_copy(k, 32).wait_send()

    @pl.when(jnp.logical_not(is_main))
    def _():
        for k in steps:
            y_copy(k, 8).wait_send()

    for copy in sum_copies:
        copy.wait_send()
    for copy, d in ((g_copies[0], 2), (g_copies[1], 1)):

        @pl.when(group + d < GROUPS)
        def _():
            copy.wait_send()

    for copy in swaps:
        copy.wait_send()


def shards(hidden, tangent, mod_shift, mod_scale, head_weight, head_bias, in_weight, in_bias, norm_gain, mid_weight):
    any_spec = pl.BlockSpec(memory_space=pl.ANY)
    dma = pltpu.SemaphoreType.DMA
    out = pl.pallas_call(
        kernel,
        out_shape=jax.ShapeDtypeStruct((TOK, CH), BF16),
        in_specs=[any_spec] * 10,
        out_specs=pl.BlockSpec(memory_space=pltpu.VMEM),
        scratch_shapes=[
            pltpu.VMEM((TOK, DS), BF16),
            pltpu.VMEM((TOK, DS), BF16),
            pltpu.VMEM((64, DS), BF16),
            pltpu.VMEM((27, 16, CH), BF16),
            pltpu.VMEM((DS,), F32),
            pltpu.VMEM((DS,), F32),
            pltpu.VMEM((64,), F32),
            pltpu.VMEM((CH,), F32),
            pltpu.VMEM((CH,), F32),
            pltpu.VMEM((TOK, 128), BF16),
            pltpu.VMEM((3, TOK, 128), BF16),
            pltpu.VMEM((8, 128), F32),
            pltpu.VMEM((3, 8, 128), F32),
            pltpu.VMEM((CG, 32, 128), BF16),
            pltpu.VMEM((CG, 32, 128), BF16),
            pltpu.VMEM((4, 32, 128), BF16),
            pltpu.VMEM((3, 4, 32, 128), BF16),
            pltpu.VMEM((576, 256), BF16),
            pltpu.VMEM((4, 768, CH), BF16),
            pltpu.VMEM((2, 4, 6, 3, 16, 256), BF16),
            pltpu.VMEM((2, 4, 2, 8, CH), F32),
            pltpu.VMEM((27, 256, CH), BF16),
            pltpu.VMEM((TOK, CH), BF16),
            pltpu.VMEM((TOK, CH), BF16),
            pltpu.SemaphoreType.REGULAR,
            pltpu.SemaphoreType.REGULAR,
            dma((11,)),
            dma,
            dma((3,)),
            dma((3,)),
            dma((3,)),
            dma((3,)),
            dma((CG,)),
            dma((CG,)),
            dma((3,)),
            dma((3,)),
            dma,
            dma,
            dma((1,)),
            dma((1,)),
        ],
        compiler_params=pltpu.CompilerParams(collective_id=0, has_side_effects=True),
        name="decode",
    )(
        hidden,
        tangent,
        mod_shift,
        mod_scale,
        head_weight,
        head_bias,
        in_weight.reshape(27, 16, CH),
        in_bias,
        norm_gain,
        mid_weight.reshape(27, SHARE, CH),
    )
    return out.reshape(1, 2, 12, 4, CH)


def solution(mesh):
    return jax.shard_map(
        shards,
        mesh=mesh,
        in_specs=(
            P("seq", "slab"),
            P("seq", "slab"),
            P("slab"),
            P("slab"),
            P(None, "slab"),
            P(),
            P(),
            P(),
            P(),
            P(None, None, None, "slab", None),
        ),
        out_specs=P("seq", None, "slab", None, None),
        check_vma=False,
    )
```
